256 devices in a mesh: row: 32 (over y, x, core), col: 8 (over z).
Axes of the slice: x: 4, y: 4, z: 8, core: 2. Of those that a mesh axis runs over, the one named last changes fastest.
Arguments:
- distances: float32 [12288, 12288], P('row', 'col'), may hold values from 0 to 4096, as said below
Outputs:
- shortest: float32 [12288, 12288], P('row', 'col')
The draws below stay inside these ranges and needn't reach their ends.
Inputs may be any that keep to these rules, and one draw needn't show every extreme that they name: `distances`: every off-diagonal entry is a whole number from 1 to 64 or the no-edge value 4096; every diagonal entry is 0.
All inputs are finite; a program needn't handle non-finite values.
Results may differ from the reference program's by a relative error of at most 0.00002.
Values sent between devices are 32-bit elements; how exact they have to be, the bound alone decides.
A program may use at most 64 MiB of HBM per device.

```python
import math
import jax
import jax.numpy as jnp
from jax import lax

N = 12288
B = 256
ROUNDS = 1


def draw_distances(key, part):
    weight_key = jax.random.fold_in(key, 11)
    edge_key = jax.random.fold_in(key, 12)
    weights = jax.random.randint(weight_key, (N, N), 1, 65)
    present = jax.random.randint(edge_key, (N, N), 0, 100) < 50
    values = jnp.where(present, weights.astype(jnp.float32), jnp.float32(4096.0))
    diagonal = lax.broadcasted_iota(jnp.int32, (N, N), 0) == lax.broadcasted_iota(jnp.int32, (N, N), 1)
    return jnp.where(diagonal, jnp.float32(0.0), values).astype(jnp.float32)


def setup_inputs(seed: int = 0) -> dict:
    key_of = jax.random.split(jax.random.key(seed), 2)
    distances = draw_distances(jax.random.fold_in(key_of[1], 71), 0)
    return dict(distances=distances)


def tropical_product(left_panel, right_panel, accumulated):
    height, inner_width = left_panel.shape
    breadth = right_panel.shape[1]
    piece_width = math.gcd(32, inner_width)
    piece_count = inner_width // piece_width
    left_pieces = left_panel.reshape(height, piece_count, piece_width).transpose(1, 0, 2)
    right_pieces = right_panel.reshape(piece_count, piece_width, breadth)

    def fold_piece(running, operands):
        left_piece, right_piece = operands
        sums = left_piece[:, :, None] + right_piece[None, :, :]
        return jnp.minimum(running, jnp.min(sums, axis=1)), None

    result, unused = lax.scan(fold_piece, accumulated, (left_pieces, right_pieces))
    return result


def close_sequential(pivot_block):
    def relax(column_index, current):
        through_col = lax.dynamic_slice_in_dim(current, column_index, 1, 1)
        through_row = lax.dynamic_slice_in_dim(current, column_index, 1, 0)
        return jnp.minimum(current, through_col + through_row)

    return lax.fori_loop(0, pivot_block.shape[0], relax, pivot_block)


def reference(distances):
    order = distances.shape[0]
    spacing = order // ROUNDS
    block_rows = math.gcd(256, order)
    current = distances
    for round_number in range(ROUNDS):
        anchor = round_number * spacing
        closed = close_sequential(current[anchor:anchor + B, anchor:anchor + B])
        row_strip = current[anchor:anchor + B, :]
        col_strip = current[:, anchor:anchor + B]
        row_panel = tropical_product(closed, row_strip, row_strip)
        col_panel = tropical_product(col_strip, closed, col_strip)

        def update_block(operands):
            return tropical_product(operands[0], row_panel, operands[1])

        blocks = lax.map(update_block, (col_panel.reshape(-1, block_rows, B), current.reshape(-1, block_rows, order)))
        current = blocks.reshape(order, order)
    return current
```

```python
import functools

import jax
import jax.numpy as jnp
from jax import lax
from jax.experimental import pallas as pl
from jax.experimental.pallas import tpu as pltpu
from jax.sharding import PartitionSpec as P

B = 256
NB = 32
MESH = pl.DeviceIdType.MESH
STEP = ((1, 0), (0, 1), (3, 0), (0, 3))
SENDS = ((0, 4, 5, 6, 8, 9, 10, 11), (4, 5), (5, 6, 7), (4, 8))


def member(value, items):
    return functools.reduce(jnp.logical_or, [value == i for i in items])


def gather_kernel(d_ref, c_ref, r_ref, p_ref, csend, crecv, rsend, rrecv, psend, precv):
    row, z = lax.axis_index("row"), lax.axis_index("col")
    core, chip = row % 2, row // 2
    x, y = chip % 4, chip // 4
    sibling = (row + 1 - 2 * core, z)
    root = chip == 0
    plus = z < 4
    minus = jnp.logical_or(z == 0, z > 5)
    up, down = (row, (z + 1) % 8), (row, (z + 7) % 8)

    def chip_at(dx, dy):
        return (2 * (((y + dy) % 4) * 4 + (x + dx) % 4) + core, z)

    def number(flag):
        return jnp.where(flag, 1, 0)

    frame = ((x, y), (y, (4 - x) % 4), ((4 - x) % 4, (4 - y) % 4), ((4 - y) % 4, x))
    forks = []
    for q in range(4):
        place = frame[q][0] * 4 + frame[q][1]
        forks.append([(member(place, SENDS[d]), chip_at(*STEP[(d + q) % 4])) for d in range(4)])

    barrier = pltpu.get_barrier_semaphore()

    def greet(device):
        pl.semaphore_signal(barrier, inc=1, device_id=device, device_id_type=MESH)

    greet(sibling)

    @pl.when(jnp.logical_and(z > 0, z < 5))
    def _():
        greet(down)

    @pl.when(z > 4)
    def _():
        greet(up)

    @pl.when(chip > 0)
    def _():
        for d in range(4):
            greet(chip_at(*STEP[d]))

    beside_root = member(chip, (1, 3, 4, 12))
    pl.semaphore_wait(barrier, 5 + number(plus) + number(minus) - number(beside_root))

    def remote(src, dst, send_sem, recv_sem, device):
        return pltpu.make_async_remote_copy(
            src_ref=src, dst_ref=dst, send_sem=send_sem, recv_sem=recv_sem, device_id=device, device_id_type=MESH
        )

    def start(flag, copy):
        @pl.when(flag)
        def _():
            copy.start()

    def finish(flag, part, send_sem, recv_sem):
        @pl.when(flag)
        def _():
            remote(part, part, send_sem, recv_sem, sibling).wait_send()

    nc = c_ref.shape[0] // NB
    width = r_ref.shape[1] // 4

    def c_part(i):
        return pl.ds(i * NB, NB), slice(0, B)

    def r_part(q, j):
        return pl.ds(j * NB, NB), slice(q * width, (q + 1) * width)

    @pl.when(z == 0)
    def _():
        for i in range(nc):
            part = c_ref.at[c_part(i)]
            pltpu.make_async_copy(d_ref.at[c_part(i)], part, crecv.at[i]).start()

    root0 = jnp.logical_and(root, core == 0)
    for j in range(B // NB):
        for q in range(4):
            part = r_part(q, j)

            @pl.when(root0)
            def _():
                pltpu.make_async_copy(d_ref.at[part], r_ref.at[part], rrecv.at[q, j]).start()

            start(root0, remote(d_ref.at[part], r_ref.at[part], rsend.at[q, j, 4], rrecv.at[q, j], sibling))

    def take_c(i):
        part = c_ref.at[c_part(i)]
        remote(part, part, csend.at[i, 0], crecv.at[i], up).wait_recv()
        start(plus, remote(part, part, csend.at[i, 0], crecv.at[i], up))
        start(minus, remote(part, part, csend.at[i, 1], crecv.at[i], down))
        if i < B // NB:

            @pl.when(root0)
            def _():
                pltpu.make_async_copy(part, p_ref.at[c_part(i)], precv.at[i]).start()

    def take_r(q, j):
        part = r_ref.at[r_part(q, j)]
        remote(part, part, rsend.at[q, j, 0], rrecv.at[q, j], sibling).wait_recv()
        for d, (flag, device) in enumerate(forks[q]):
            start(jnp.logical_and(core == 1, flag), remote(part, part, rsend.at[q, j, d], rrecv.at[q, j], device))
        start(
            jnp.logical_and(core == 1, chip > 0),
            remote(part, part, rsend.at[q, j, 4], rrecv.at[q, j], sibling),
        )

    def take_p(i):
        part = p_ref.at[c_part(i)]
        remote(part, part, psend.at[i, 0], precv.at[i], sibling).wait_recv()
        for d, (flag, device) in enumerate(forks[i % 4]):
            start(jnp.logical_and(core == 0, flag), remote(part, part, psend.at[i, d], precv.at[i], device))
        start(core == 0, remote(part, part, psend.at[i, 4], precv.at[i], sibling))

    n = B // NB

    @pl.when(core == 0)
    def _():
        for i in range(n):
            take_c(i)
        for i in range(n):
            take_p(i)
            if i % 2 == 1:
                take_c(n + i // 2)
        for j in range(n):
            for q in range(4):
                take_r(q, j)

    @pl.when(core == 1)
    def _():
        for j in range(n):
            for q in range(4):
                take_r(q, j)
            take_c(j)
        for i in range(n, nc):
            take_c(i)
        for i in range(n):
            take_p(i)

    for i in range(nc):
        part = c_ref.at[c_part(i)]
        finish(plus, part, csend.at[i, 0], crecv.at[i])
        finish(minus, part, csend.at[i, 1], crecv.at[i])
    for j in range(n):
        for q in range(4):
            part = r_ref.at[r_part(q, j)]
            for d in range(4):
                finish(jnp.logical_and(core == 1, forks[q][d][0]), part, rsend.at[q, j, d], rrecv.at[q, j])
            own = jnp.logical_or(root0, jnp.logical_and(core == 1, chip > 0))
            finish(own, part, rsend.at[q, j, 4], rrecv.at[q, j])
    for i in range(n):
        part = p_ref.at[c_part(i)]
        for d in range(4):
            finish(jnp.logical_and(core == 0, forks[i % 4][d][0]), part, psend.at[i, d], precv.at[i])
        finish(core == 0, part, psend.at[i, 4], precv.at[i])


def gather(distances):
    rows, cols = distances.shape
    f32 = jnp.float32
    return pl.pallas_call(
        gather_kernel,
        out_shape=(
            jax.ShapeDtypeStruct((rows, B), f32),
            jax.ShapeDtypeStruct((B, cols), f32),
            jax.ShapeDtypeStruct((B, B), f32),
        ),
        in_specs=[pl.BlockSpec(memory_space=pl.ANY)],
        out_specs=[pl.BlockSpec(memory_space=pltpu.VMEM)] * 3,
        scratch_shapes=[
            pltpu.SemaphoreType.DMA((rows // NB, 2)),
            pltpu.SemaphoreType.DMA((rows // NB,)),
            pltpu.SemaphoreType.DMA((4, B // NB, 5)),
            pltpu.SemaphoreType.DMA((4, B // NB)),
            pltpu.SemaphoreType.DMA((B // NB, 5)),
            pltpu.SemaphoreType.DMA((B // NB,)),
        ],
        compiler_params=pltpu.CompilerParams(collective_id=0, has_side_effects=True),
        name="gather",
    )(distances)


def panel_update(x_ref, row0, rows, panel_ref, k, group):
    def step(g, carry):
        part = pl.ds(pl.multiple_of(row0 + g * group, 8), group)
        value = x_ref[part, :]
        left = x_ref[part, k : k + NB]
        for l in range(NB):
            value = jnp.minimum(value, left[:, l : l + 1] + panel_ref[k + l : k + l + 1, :])
        x_ref[part, :] = value
        return carry

    lax.fori_loop(0, rows // group, step, 0)


def close_and_extend(pivot_ref, panel_ref, x_ref):
    for k in range(0, B, NB):
        here = k // 128 * 128
        other = 128 - here
        rows = pl.ds(k, NB)
        square = pivot_ref[rows, here : here + 128]
        panel_ref[rows, here : here + 128] = square
        for _ in range(5):
            left = square[:, k - here : k - here + NB]
            for l in range(NB):
                square = jnp.minimum(square, left[:, l : l + 1] + panel_ref[k + l : k + l + 1, here : here + 128])
            panel_ref[rows, here : here + 128] = square
        left = square[:, k - here : k - here + NB]
        value = pivot_ref[rows, other : other + 128]
        for l in range(NB):
            value = jnp.minimum(value, left[:, l : l + 1] + pivot_ref[k + l : k + l + 1, other : other + 128])
        panel_ref[rows, other : other + 128] = value
        if k + NB < B:
            panel_update(pivot_ref, k + NB, B - k - NB, panel_ref, k, 32)
        panel_update(x_ref, 0, x_ref.shape[0], panel_ref, k, 64)


TI, TJ, U = 24, 512, 32


def min_plus(x_ref, y_ref, acc_ref, out_ref, wide_ref):
    height, depth = x_ref.shape
    breadth = y_ref.shape[1]
    blocks, strips = height // TI, breadth // TJ
    share = 8 * (-(-(TI // 8) // strips))

    def widen(slot, left, row0, l0):
        for u in range(U):
            wide_ref[slot, l0 + u, row0 : row0 + share, :] = jnp.broadcast_to(left[:, u : u + 1], (share, 128))
        return pltpu.roll(left, 128 - U, 1)

    for s in range(TI // share):
        for half in range(depth // 128):

            def first(g, left):
                return widen(0, left, s * share, pl.multiple_of(half * 128 + g * U, U))

            lax.fori_loop(0, 128 // U, first, x_ref[s * share : (s + 1) * share, half * 128 : half * 128 + 128])

    def block(b, carry):
        slot = lax.rem(b, 2)
        row0 = pl.multiple_of(b * TI, TI)
        next0 = pl.multiple_of(jnp.minimum(b + 1, blocks - 1) * TI, TI)
        for s in range(strips):
            strip = slice(s * TJ, (s + 1) * TJ)
            value = acc_ref[pl.ds(row0, TI), strip]
            for half in range(depth // 128):

                def group(g, state):
                    value, left = state
                    l0 = pl.multiple_of(half * 128 + g * U, U)
                    right = y_ref.at[pl.ds(l0, U), strip]
                    for u in range(U):
                        wide = wide_ref[slot, l0 + u]
                        row = right[pl.ds(u, 8, stride=0), :]
                        value = jnp.concatenate(
                            [
                                jnp.minimum(
                                    value[:, c : c + 128], wide + jnp.concatenate([row[:, c : c + 128]] * (TI // 8), 0)
                                )
                                for c in range(0, TJ, 128)
                            ],
                            1,
                        )
                    if s * share < TI:
                        left = widen(1 - slot, left, s * share, l0)
                    return value, left

                left = x_ref[pl.ds(next0 + s * share, share), half * 128 : half * 128 + 128]
                value, left = lax.fori_loop(0, 128 // U, group, (value, left))
            out_ref[pl.ds(row0, TI), strip] = value
        return carry

    lax.fori_loop(0, blocks, block, 0)


def update_kernel(c_ref, r_ref, p_ref, d_ref, out_ref, x_ref, pivot_ref, panel_ref, wide_ref):
    pivot_ref[...] = p_ref[...]
    x_ref[...] = c_ref[...]
    close_and_extend(pivot_ref, panel_ref, x_ref)
    min_plus(x_ref, r_ref, d_ref, out_ref, wide_ref)


def on_device(distances):
    rows, cols = distances.shape
    f32 = jnp.float32
    c, r, p = gather(distances)
    return pl.pallas_call(
        update_kernel,
        out_shape=jax.ShapeDtypeStruct((rows, cols), f32),
        in_specs=[pl.BlockSpec(memory_space=pltpu.VMEM)] * 4,
        out_specs=pl.BlockSpec(memory_space=pltpu.VMEM),
        scratch_shapes=[
            pltpu.VMEM((rows, B), f32),
            pltpu.VMEM((B, B), f32),
            pltpu.VMEM((B, B), f32),
            pltpu.VMEM((2, B, TI, 128), f32),
        ],
        name="update",
    )(c, r, p, distances)


def solution(mesh):
    spec = P("row", "col")
    return jax.shard_map(on_device, mesh=mesh, in_specs=(spec,), out_specs=spec, check_vma=False)
```

```python
import functools

import jax
import jax.numpy as jnp
from jax import lax
from jax.experimental import pallas as pl
from jax.experimental.pallas import tpu as pltpu
from jax.sharding import PartitionSpec as P

B = 256
NB = 32
MESH = pl.DeviceIdType.MESH
STEP = ((1, 0), (0, 1), (3, 0), (0, 3))
SENDS = ((0, 4, 5, 6, 8, 9, 10, 11), (4, 5), (5, 6, 7), (4, 8))
DEPTHS = ((0,), (4,), (5, 7, 8), (1, 6, 9, 3, 11, 12), (2, 10, 13, 15), (14,))
HOP = 4


def member(value, items):
    return functools.reduce(jnp.logical_or, [value == i for i in items])


def gather_kernel(d_ref, c_ref, r_ref, p_ref, csend, crecv, rsend, rrecv, psend, precv):
    row, z = lax.axis_index("row"), lax.axis_index("col")
    core, chip = row % 2, row // 2
    x, y = chip % 4, chip // 4
    sibling = (row + 1 - 2 * core, z)
    root = chip == 0
    plus = z < 4
    minus = jnp.logical_or(z == 0, z > 5)
    up, down = (row, (z + 1) % 8), (row, (z + 7) % 8)

    def chip_at(dx, dy):
        return (2 * (((y + dy) % 4) * 4 + (x + dx) % 4) + core, z)

    def number(flag):
        return jnp.where(flag, 1, 0)

    frame = ((x, y), (y, (4 - x) % 4), ((4 - x) % 4, (4 - y) % 4), ((4 - y) % 4, x))
    forks = []
    for q in range(4):
        place = frame[q][0] * 4 + frame[q][1]
        forks.append([(member(place, SENDS[d]), chip_at(*STEP[(d + q) % 4])) for d in range(4)])

    barrier = pltpu.get_barrier_semaphore()

    def greet(device):
        pl.semaphore_signal(barrier, inc=1, device_id=device, device_id_type=MESH)

    greet(sibling)

    @pl.when(jnp.logical_and(z > 0, z < 5))
    def _():
        greet(down)

    @pl.when(z > 4)
    def _():
        greet(up)

    @pl.when(chip > 0)
    def _():
        for d in range(4):
            greet(chip_at(*STEP[d]))

    beside_root = member(chip, (1, 3, 4, 12))
    pl.semaphore_wait(barrier, 5 + number(plus) + number(minus) - number(beside_root))

    def remote(src, dst, send_sem, recv_sem, device):
        return pltpu.make_async_remote_copy(
            src_ref=src, dst_ref=dst, send_sem=send_sem, recv_sem=recv_sem, device_id=device, device_id_type=MESH
        )

    def start(flag, copy):
        @pl.when(flag)
        def _():
            copy.start()

    def finish(flag, part, send_sem, recv_sem):
        @pl.when(flag)
        def _():
            remote(part, part, send_sem, recv_sem, sibling).wait_send()

    nc = c_ref.shape[0] // NB
    width = r_ref.shape[1] // 4

    def c_part(i):
        return pl.ds(pl.multiple_of(i * NB, NB), NB), slice(0, B)

    def r_part(q, j):
        return pl.ds(pl.multiple_of(j * NB, NB), NB), slice(q * width, (q + 1) * width)

    @pl.when(z == 0)
    def _():
        for i in range(nc):
            part = c_ref.at[c_part(i)]
            pltpu.make_async_copy(d_ref.at[c_part(i)], part, crecv.at[i]).start()

    root0 = jnp.logical_and(root, core == 0)

    @pl.when(root0)
    def _():
        @pl.loop(0, B // NB)
        def _(j):
            for q in range(4):
                part = r_part(q, j)
                pltpu.make_async_copy(d_ref.at[part], r_ref.at[part], rrecv.at[q, j]).start()
                remote(d_ref.at[part], r_ref.at[part], rsend.at[q, j, 4], rrecv.at[q, j], sibling).start()

    n = B // NB
    reach = jnp.where(z < 5, z, 8 - z)
    depth = []
    for q in range(4):
        place = frame[q][0] * 4 + frame[q][1]
        depth.append(sum(number(member(place, DEPTHS[k])) * k for k in range(1, 6)))

    def take_c(i):
        part = c_ref.at[c_part(i)]
        remote(part, part, csend.at[i, 0], crecv.at[i], up).wait_recv()
        start(plus, remote(part, part, csend.at[i, 0], crecv.at[i], up))
        start(minus, remote(part, part, csend.at[i, 1], crecv.at[i], down))

        @pl.when(jnp.logical_and(root0, i < n))
        def _():
            pltpu.make_async_copy(part, p_ref.at[c_part(i)], precv.at[i]).start()

    def take_r(q, j):
        part = r_ref.at[r_part(q, j)]
        remote(part, part, rsend.at[q, j, 0], rrecv.at[q, j], sibling).wait_recv()
        for d, (flag, device) in enumerate(forks[q]):
            start(flag, remote(part, part, rsend.at[q, j, d], rrecv.at[q, j], device))
        start(chip > 0, remote(part, part, rsend.at[q, j, 4], rrecv.at[q, j], sibling))

    def take_p(i):
        part = p_ref.at[c_part(i)]
        remote(part, part, psend.at[i, 0], precv.at[i], sibling).wait_recv()
        for d, (flag, device) in enumerate(forks[i % 4]):
            start(flag, remote(part, part, psend.at[i, d], precv.at[i], device))
        start(True, remote(part, part, psend.at[i, 4], precv.at[i], sibling))

    @pl.loop(0, 5 * HOP + 4 * HOP + 3 * nc // 2 + 2)
    def _(t):
        u = t - HOP * reach
        i = (2 * u + u % 3) // 3

        @pl.when(jnp.logical_and(jnp.logical_and(u >= 0, u % 3 < 2), i < nc))
        def _():
            take_c(i)

        @pl.when(core == 0)
        def _():
            for i in range(n):

                @pl.when(u == 3 * i // 2 + 1 + HOP * depth[i % 4])
                def _():
                    take_p(i)

        @pl.when(core == 1)
        def _():
            for q in range(4):
                j = t - HOP * depth[q]

                @pl.when(jnp.logical_and(j >= 0, j < n))
                def _():
                    take_r(q, j)

    @pl.when(core == 0)
    def _():
        @pl.loop(0, n)
        def _(j):
            for q in range(4):
                part = r_ref.at[r_part(q, j)]
                remote(part, part, rsend.at[q, j, 0], rrecv.at[q, j], sibling).wait_recv()

    @pl.when(core == 1)
    def _():
        @pl.loop(0, n)
        def _(i):
            part = p_ref.at[c_part(i)]
            remote(part, part, psend.at[i, 0], precv.at[i], sibling).wait_recv()

    @pl.loop(0, nc)
    def _(i):
        part = c_ref.at[c_part(i)]
        finish(plus, part, csend.at[i, 0], crecv.at[i])
        finish(minus, part, csend.at[i, 1], crecv.at[i])

    @pl.loop(0, n)
    def _(j):
        for q in range(4):
            part = r_ref.at[r_part(q, j)]
            for d in range(4):
                finish(jnp.logical_and(core == 1, forks[q][d][0]), part, rsend.at[q, j, d], rrecv.at[q, j])
            own = jnp.logical_or(root0, jnp.logical_and(core == 1, chip > 0))
            finish(own, part, rsend.at[q, j, 4], rrecv.at[q, j])

    for i in range(n):
        part = p_ref.at[c_part(i)]
        for d in range(4):
            finish(jnp.logical_and(core == 0, forks[i % 4][d][0]), part, psend.at[i, d], precv.at[i])
        finish(core == 0, part, psend.at[i, 4], precv.at[i])


def gather(distances):
    rows, cols = distances.shape
    f32 = jnp.float32
    return pl.pallas_call(
        gather_kernel,
        out_shape=(
            jax.ShapeDtypeStruct((rows, B), f32),
            jax.ShapeDtypeStruct((B, cols), f32),
            jax.ShapeDtypeStruct((B, B), f32),
        ),
        in_specs=[pl.BlockSpec(memory_space=pl.ANY)],
        out_specs=[pl.BlockSpec(memory_space=pltpu.VMEM)] * 3,
        scratch_shapes=[
            pltpu.SemaphoreType.DMA((rows // NB, 2)),
            pltpu.SemaphoreType.DMA((rows // NB,)),
            pltpu.SemaphoreType.DMA((4, B // NB, 5)),
            pltpu.SemaphoreType.DMA((4, B // NB)),
            pltpu.SemaphoreType.DMA((B // NB, 5)),
            pltpu.SemaphoreType.DMA((B // NB,)),
        ],
        compiler_params=pltpu.CompilerParams(collective_id=0, has_side_effects=True),
        name="gather",
    )(distances)


def panel_update(x_ref, row0, rows, panel_ref, k, group):
    def step(g, carry):
        part = pl.ds(pl.multiple_of(row0 + g * group, 8), group)
        value = x_ref[part, :]
        left = x_ref[part, k : k + NB]
        for l in range(NB):
            value = jnp.minimum(value, left[:, l : l + 1] + panel_ref[k + l : k + l + 1, :])
        x_ref[part, :] = value
        return carry

    lax.fori_loop(0, rows // group, step, 0)


def close_and_extend(pivot_ref, panel_ref, x_ref):
    for k in range(0, B, NB):
        here = k // 128 * 128
        other = 128 - here
        rows = pl.ds(k, NB)
        square = pivot_ref[rows, here : here + 128]
        panel_ref[rows, here : here + 128] = square
        for _ in range(5):
            left = square[:, k - here : k - here + NB]
            for l in range(NB):
                square = jnp.minimum(square, left[:, l : l + 1] + panel_ref[k + l : k + l + 1, here : here + 128])
            panel_ref[rows, here : here + 128] = square
        left = square[:, k - here : k - here + NB]
        value = pivot_ref[rows, other : other + 128]
        for l in range(NB):
            value = jnp.minimum(value, left[:, l : l + 1] + pivot_ref[k + l : k + l + 1, other : other + 128])
        panel_ref[rows, other : other + 128] = value
        if k + NB < B:
            panel_update(pivot_ref, k + NB, B - k - NB, panel_ref, k, 32)
        panel_update(x_ref, 0, x_ref.shape[0], panel_ref, k, 64)


TI, TJ, U = 24, 512, 32


def min_plus(x_ref, y_ref, acc_ref, out_ref, wide_ref):
    height, depth = x_ref.shape
    breadth = y_ref.shape[1]
    blocks, strips = height // TI, breadth // TJ
    share = 8 * (-(-(TI // 8) // strips))

    def widen(slot, left, row0, l0):
        for u in range(U):
            wide_ref[slot, l0 + u, row0 : row0 + share, :] = jnp.broadcast_to(left[:, u : u + 1], (share, 128))
        return pltpu.roll(left, 128 - U, 1)

    for s in range(TI // share):
        for half in range(depth // 128):

            def first(g, left):
                return widen(0, left, s * share, pl.multiple_of(half * 128 + g * U, U))

            lax.fori_loop(0, 128 // U, first, x_ref[s * share : (s + 1) * share, half * 128 : half * 128 + 128])

    def block(b, carry):
        slot = lax.rem(b, 2)
        row0 = pl.multiple_of(b * TI, TI)
        next0 = pl.multiple_of(jnp.minimum(b + 1, blocks - 1) * TI, TI)
        for s in range(strips):
            strip = slice(s * TJ, (s + 1) * TJ)
            value = acc_ref[pl.ds(row0, TI), strip]
            for half in range(depth // 128):

                def group(g, state):
                    value, left = state
                    l0 = pl.multiple_of(half * 128 + g * U, U)
                    right = y_ref.at[pl.ds(l0, U), strip]
                    for u in range(U):
                        wide = wide_ref[slot, l0 + u]
                        row = right[pl.ds(u, 8, stride=0), :]
                        value = jnp.concatenate(
                            [
                                jnp.minimum(
                                    value[:, c : c + 128], wide + jnp.concatenate([row[:, c : c + 128]] * (TI // 8), 0)
                                )
                                for c in range(0, TJ, 128)
                            ],
                            1,
                        )
                    if s * share < TI:
                        left = widen(1 - slot, left, s * share, l0)
                    return value, left

                left = x_ref[pl.ds(next0 + s * share, share), half * 128 : half * 128 + 128]
                value, left = lax.fori_loop(0, 128 // U, group, (value, left))
            out_ref[pl.ds(row0, TI), strip] = value
        return carry

    lax.fori_loop(0, blocks, block, 0)


def update_kernel(c_ref, r_ref, p_ref, d_ref, out_ref, x_ref, pivot_ref, panel_ref, wide_ref):
    pivot_ref[...] = p_ref[...]
    x_ref[...] = c_ref[...]
    close_and_extend(pivot_ref, panel_ref, x_ref)
    min_plus(x_ref, r_ref, d_ref, out_ref, wide_ref)


def on_device(distances):
    rows, cols = distances.shape
    f32 = jnp.float32
    c, r, p = gather(distances)
    return pl.pallas_call(
        update_kernel,
        out_shape=jax.ShapeDtypeStruct((rows, cols), f32),
        in_specs=[pl.BlockSpec(memory_space=pltpu.VMEM)] * 4,
        out_specs=pl.BlockSpec(memory_space=pltpu.VMEM),
        scratch_shapes=[
            pltpu.VMEM((rows, B), f32),
            pltpu.VMEM((B, B), f32),
            pltpu.VMEM((B, B), f32),
            pltpu.VMEM((2, B, TI, 128), f32),
        ],
        name="update",
    )(c, r, p, distances)


def solution(mesh):
    spec = P("row", "col")
    return jax.shard_map(on_device, mesh=mesh, in_specs=(spec,), out_specs=spec, check_vma=False)
```

```python
import functools

import jax
import jax.numpy as jnp
from jax import lax
from jax.experimental import pallas as pl
from jax.experimental.pallas import tpu as pltpu
from jax.sharding import PartitionSpec as P

B = 256
NB = 32
KB = 16
MESH = pl.DeviceIdType.MESH
STEP = ((1, 0), (0, 1), (3, 0), (0, 3))
SENDS = ((0, 4, 5, 6, 8, 9, 10, 11), (4, 5), (5, 6, 7), (4, 8))
DEPTHS = ((0,), (4,), (5, 7, 8), (1, 6, 9, 3, 11, 12), (2, 10, 13, 15), (14,))
TAKES = ((4, 8, 9, 10, 12, 13, 14, 15), (5, 6), (1, 2, 3), (7, 11))
HOP = 4


def member(value, items):
    return functools.reduce(jnp.logical_or, [value == i for i in items])


def gather_kernel(d_ref, c_ref, r_ref, p_ref, csend, crecv, rsend, rrecv, psend, precv):
    row, z = lax.axis_index("row"), lax.axis_index("col")
    core, chip = row % 2, row // 2
    x, y = chip % 4, chip // 4
    sibling = (row + 1 - 2 * core, z)
    root = row == 0
    plus = z < 4
    minus = jnp.logical_or(z == 0, z > 5)
    up, down = (row, (z + 1) % 8), (row, (z + 7) % 8)
    n, nc = B // NB, c_ref.shape[0] // NB
    width = r_ref.shape[1] // 4

    def number(flag):
        return jnp.where(flag, 1, 0)

    def both(*flags):
        return functools.reduce(jnp.logical_and, flags)

    def chip_at(step, side):
        dx, dy = step
        return (2 * (((y + dy) % 4) * 4 + (x + dx) % 4) + side, z)

    frame = ((x, y), (y, (4 - x) % 4), ((4 - x) % 4, (4 - y) % 4), ((4 - y) % 4, x))
    forks, depth, mine = [], [], []
    barrier = pltpu.get_barrier_semaphore()

    def greet(device):
        pl.semaphore_signal(barrier, inc=1, device_id=device, device_id_type=MESH)

    expected = 1 + number(plus) + number(minus)
    for q in range(4):
        side = q // 2
        place = frame[q][0] * 4 + frame[q][1]
        mine.append(both(chip > 0, core == side))
        carries = jnp.logical_or(root, mine[q])
        forks.append([])
        for d in range(4):
            step = STEP[(d + q) % 4]
            flag = both(carries, member(place, SENDS[d]))
            forks[q].append((flag, chip_at(step, side)))
            expected = expected + number(flag)
            back = (4 - step[0]) % 4, (4 - step[1]) % 4

            @pl.when(both(mine[q], member(place, TAKES[d])))
            def _():
                source, at = chip_at(back, side)
                greet((jnp.where(source < 2, 0, source), at))

        depth.append(sum(number(member(place, DEPTHS[k])) * k for k in range(1, 6)))

    greet(sibling)

    @pl.when(both(z > 0, z < 5))
    def _():
        greet(down)

    @pl.when(z > 4)
    def _():
        greet(up)

    pl.semaphore_wait(barrier, expected)

    def remote(src, dst, send_sem, recv_sem, device):
        return pltpu.make_async_remote_copy(
            src_ref=src, dst_ref=dst, send_sem=send_sem, recv_sem=recv_sem, device_id=device, device_id_type=MESH
        )

    def start(flag, copy):
        @pl.when(flag)
        def _():
            copy.start()

    def finish(flag, part, send_sem, recv_sem):
        @pl.when(flag)
        def _():
            remote(part, part, send_sem, recv_sem, sibling).wait_send()

    def await_part(part, send_sem, recv_sem):
        remote(part, part, send_sem, recv_sem, sibling).wait_recv()

    def c_part(i):
        return pl.ds(pl.multiple_of(i * NB, NB), NB), slice(0, B)

    def r_part(q, j):
        return pl.ds(pl.multiple_of(j * NB, NB), NB), slice(q * width, (q + 1) * width)

    @pl.when(z == 0)
    def _():
        @pl.loop(0, nc)
        def _(i):
            pltpu.make_async_copy(d_ref.at[c_part(i)], c_ref.at[c_part(i)], crecv.at[i]).start()

    @pl.when(root)
    def _():
        @pl.loop(0, n)
        def _(j):
            for q in range(4):
                part = r_part(q, j)
                pltpu.make_async_copy(d_ref.at[part], r_ref.at[part], rrecv.at[q, j]).start()

    def take_c(i):
        part = c_ref.at[c_part(i)]
        await_part(part, csend.at[i, 0], crecv.at[i])
        start(plus, remote(part, part, csend.at[i, 0], crecv.at[i], up))
        start(minus, remote(part, part, csend.at[i, 1], crecv.at[i], down))

        @pl.when(both(root, i < n))
        def _():
            pltpu.make_async_copy(part, p_ref.at[c_part(i)], precv.at[i]).start()

    def take_r(q, j):
        part = r_ref.at[r_part(q, j)]
        await_part(part, rsend.at[q, j, 0], rrecv.at[q, j])
        for d, (flag, device) in enumerate(forks[q]):
            start(flag, remote(part, part, rsend.at[q, j, d], rrecv.at[q, j], device))
        remote(part, part, rsend.at[q, j, 4], rrecv.at[q, j], sibling).start()

    def take_p(i):
        part = p_ref.at[c_part(i)]
        await_part(part, psend.at[i, 0], precv.at[i])
        for d, (flag, device) in enumerate(forks[i % 4]):
            start(flag, remote(part, part, psend.at[i, d], precv.at[i], device))
        remote(part, part, psend.at[i, 4], precv.at[i], sibling).start()

    carrying = [jnp.logical_or(root, mine[q]) for q in range(4)]

    reach = jnp.where(z < 5, z, 8 - z)

    @pl.loop(0, 5 * HOP + 4 * HOP + 3 * nc // 2 + 2)
    def _(t):
        u = t - HOP * reach
        i = (2 * u + u % 3) // 3

        @pl.when(both(u >= 0, u % 3 < 2, i < nc))
        def _():
            take_c(i)

        for i in range(n):

            @pl.when(both(carrying[i % 4], u == 3 * i // 2 + 1 + HOP * depth[i % 4]))
            def _():
                take_p(i)

        for q in range(4):
            j = t - HOP * depth[q]

            @pl.when(both(carrying[q], j >= 0, j < n))
            def _():
                take_r(q, j)

    @pl.loop(0, n)
    def _(j):
        for q in range(4):
            part = r_ref.at[r_part(q, j)]

            @pl.when(jnp.logical_not(carrying[q]))
            def _():
                await_part(part, rsend.at[q, j, 0], rrecv.at[q, j])

            for d in range(4):
                finish(forks[q][d][0], part, rsend.at[q, j, d], rrecv.at[q, j])
            finish(carrying[q], part, rsend.at[q, j, 4], rrecv.at[q, j])

    @pl.loop(0, nc)
    def _(i):
        part = c_ref.at[c_part(i)]
        finish(plus, part, csend.at[i, 0], crecv.at[i])
        finish(minus, part, csend.at[i, 1], crecv.at[i])

    for i in range(n):
        q = i % 4
        part = p_ref.at[c_part(i)]

        @pl.when(jnp.logical_not(carrying[q]))
        def _():
            await_part(part, psend.at[i, 0], precv.at[i])

        for d in range(4):
            finish(forks[q][d][0], part, psend.at[i, d], precv.at[i])
        finish(carrying[q], part, psend.at[i, 4], precv.at[i])


def gather(distances):
    rows, cols = distances.shape
    f32 = jnp.float32
    return pl.pallas_call(
        gather_kernel,
        out_shape=(
            jax.ShapeDtypeStruct((rows, B), f32),
            jax.ShapeDtypeStruct((B, cols), f32),
            jax.ShapeDtypeStruct((B, B), f32),
        ),
        in_specs=[pl.BlockSpec(memory_space=pl.ANY)],
        out_specs=[pl.BlockSpec(memory_space=pltpu.VMEM)] * 3,
        scratch_shapes=[
            pltpu.SemaphoreType.DMA((rows // NB, 2)),
            pltpu.SemaphoreType.DMA((rows // NB,)),
            pltpu.SemaphoreType.DMA((4, B // NB, 5)),
            pltpu.SemaphoreType.DMA((4, B // NB)),
            pltpu.SemaphoreType.DMA((B // NB, 5)),
            pltpu.SemaphoreType.DMA((B // NB,)),
        ],
        compiler_params=pltpu.CompilerParams(collective_id=0, has_side_effects=True),
        name="gather",
    )(distances)


def close_and_extend(p_ref, c_ref, z_refs, wide_refs, panel_refs, old_ref, square_ref, hot_ref):
    strips = len(z_refs)
    left_strips = B // 128
    for r in range(0, B, 128):
        for t in range(left_strips):
            z_refs[t][r : r + 128, :] = p_ref[t * 128 : t * 128 + 128, r : r + 128].T
        for t in range(strips - left_strips):
            z_refs[left_strips + t][r : r + 128, :] = c_ref[t * 128 : t * 128 + 128, r : r + 128].T
    rows = lax.broadcasted_iota(jnp.int32, (B, 128), 0) % 128
    for l in range(KB):
        hot_ref[:, l * 128 : l * 128 + 128] = jnp.where(rows == l, 1.0, 0.0).astype(jnp.bfloat16)

    def lanes(t):
        return slice(t * 128, t * 128 + 128)

    def spread(ref, row, t):
        view = ref.at[row // 8 * 8 : row // 8 * 8 + 8, lanes(t)]
        line = view[pl.ds(row % 8, 8, stride=0), :]
        return jnp.concatenate([line] * (KB // 8), 0)

    def block(k):
        return pl.ds(pl.multiple_of(k, KB), KB)

    def turn(value, k):
        return pltpu.roll(value, lax.rem(128 - lax.rem(k, 128), 128), 1)

    def widen(slot, k, first):
        column = turn(z_refs[first][...], k)
        high = jnp.floor(column * (1 / 32)) * 32
        split = jnp.concatenate([high, column - high], 1).astype(jnp.bfloat16)
        for c in range(0, KB * 128, 512):
            wide_refs[slot][:, c : c + 512] = jnp.dot(split, hot_ref[:, c : c + 512], preferred_element_type=jnp.float32)

    def close(slot, k, first, tiles):
        square = turn(old_ref[:, lanes(first)], k)
        for step in range(KB.bit_length() - 1):
            square_ref[step] = square
            left = square[:, :KB]
            for l in range(KB):
                square = jnp.minimum(square, left[:, l : l + 1] + spread(square_ref.at[step], l, 0))
        values = [old_ref[:, lanes(t)] for t in tiles]
        for l in range(KB):
            column = jnp.broadcast_to(square[:, l : l + 1], (KB, 128))
            values = [jnp.minimum(v, column + spread(old_ref, l, t)) for v, t in zip(values, tiles)]
        for v, t in zip(values, tiles):
            panel_refs[slot][:, lanes(t)] = v

    def through(slot, starts, tiles):
        values = [[z_refs[t][block(r), :] for t in tiles] for r in starts]
        for l in range(KB):
            lines = [spread(panel_refs[slot], l, t) for t in tiles]
            for n, r in enumerate(starts):
                column = wide_refs[slot][block(r), lanes(l)]
                values[n] = [jnp.minimum(v, column + line) for v, line in zip(values[n], lines)]
        return values

    def update(slot, starts, tiles):
        for r, row in zip(starts, through(slot, starts, tiles)):
            for t, value in zip(tiles, row):
                z_refs[t][block(r), :] = value

    right = list(range(left_strips, strips))

    def stage(slot, k, first, others):
        after = k + KB
        rest = [lax.rem(after + r, B) for r in range(KB, B - KB, KB)]
        live = [first] + others
        for t, value in zip(live, through(slot, [after], live)[0]):
            old_ref[:, lanes(t)] = value
        update(slot, rest, [first])
        close(1 - slot, after, first, live)
        widen(1 - slot, after, first)
        for r in rest:
            update(slot, [r], others)
        for t in live:
            z_refs[t][block(after), :] = panel_refs[1 - slot][:, lanes(t)]

    def pair(start, first, others):
        def run(i, carry):
            k = start + i * (2 * KB)
            stage(1, k, first, others)
            stage(0, k + KB, first, others)
            return carry

        return run

    widen(0, 0, 0)
    for t in range(strips):
        old_ref[:, lanes(t)] = z_refs[t][0:KB, :]
    close(0, 0, 0, list(range(strips)))
    for t in range(strips):
        z_refs[t][0:KB, :] = panel_refs[0][:, lanes(t)]
    stage(0, 0, 0, [1] + right)
    lax.fori_loop(0, 3, pair(KB, 0, [1] + right), 0)
    lax.fori_loop(0, 4, pair(128 - KB, 1, right), 0)
    for r in range(0, B - KB, KB):
        update(1, [r], right)
    for t in range(strips - left_strips):
        for r in range(0, B, 128):
            c_ref[t * 128 : t * 128 + 128, r : r + 128] = z_refs[left_strips + t][r : r + 128, :].T


TI, TJ, U = 24, 512, 32


def min_plus(x_ref, y_ref, acc_ref, out_ref, wide_ref):
    height, depth = x_ref.shape
    breadth = y_ref.shape[1]
    blocks, strips = height // TI, breadth // TJ
    share = 8 * (-(-(TI // 8) // strips))

    def widen(slot, left, row0, l0):
        for u in range(U):
            wide_ref[slot, l0 + u, row0 : row0 + share, :] = jnp.broadcast_to(left[:, u : u + 1], (share, 128))
        return pltpu.roll(left, 128 - U, 1)

    for s in range(TI // share):
        for half in range(depth // 128):

            def first(g, left):
                return widen(0, left, s * share, pl.multiple_of(half * 128 + g * U, U))

            lax.fori_loop(0, 128 // U, first, x_ref[s * share : (s + 1) * share, half * 128 : half * 128 + 128])

    def block(b, carry):
        slot = lax.rem(b, 2)
        row0 = pl.multiple_of(b * TI, TI)
        next0 = pl.multiple_of(jnp.minimum(b + 1, blocks - 1) * TI, TI)
        for s in range(strips):
            strip = slice(s * TJ, (s + 1) * TJ)
            value = acc_ref[pl.ds(row0, TI), strip]
            for half in range(depth // 128):

                def group(g, state):
                    value, left = state
                    l0 = pl.multiple_of(half * 128 + g * U, U)
                    right = y_ref.at[pl.ds(l0, U), strip]
                    for u in range(U):
                        wide = wide_ref[slot, l0 + u]
                        row = right[pl.ds(u, 8, stride=0), :]
                        value = jnp.concatenate(
                            [
                                jnp.minimum(
                                    value[:, c : c + 128], wide + jnp.concatenate([row[:, c : c + 128]] * (TI // 8), 0)
                                )
                                for c in range(0, TJ, 128)
                            ],
                            1,
                        )
                    if s * share < TI:
                        left = widen(1 - slot, left, s * share, l0)
                    return value, left

                left = x_ref[pl.ds(next0 + s * share, share), half * 128 : half * 128 + 128]
                value, left = lax.fori_loop(0, 128 // U, group, (value, left))
            out_ref[pl.ds(row0, TI), strip] = value
        return carry

    lax.fori_loop(0, blocks, block, 0)


def update_kernel(c_ref, r_ref, p_ref, d_ref, out_ref, x_ref, old_ref, square_ref, hot_ref, wide_ref, *more):
    x_ref[...] = c_ref[...]
    close_and_extend(p_ref, x_ref, more[4:], more[:2], more[2:4], old_ref, square_ref, hot_ref)
    min_plus(x_ref, r_ref, d_ref, out_ref, wide_ref)


def scratch(rows):
    f32 = jnp.float32
    width = B + rows
    return [
        pltpu.VMEM((rows, B), f32),
        pltpu.VMEM((KB, width), f32),
        pltpu.VMEM((KB.bit_length(), KB, 128), f32),
        pltpu.VMEM((B, KB * 128), jnp.bfloat16),
        pltpu.VMEM((2, B, TI, 128), f32),
        *[pltpu.VMEM((B, KB * 128), f32)] * 2,
        *[pltpu.VMEM((KB, width), f32)] * 2,
        *[pltpu.VMEM((B, 128), f32)] * (width // 128),
    ]


def on_device(distances):
    rows, cols = distances.shape
    f32 = jnp.float32
    c, r, p = gather(distances)
    return pl.pallas_call(
        update_kernel,
        out_shape=jax.ShapeDtypeStruct((rows, cols), f32),
        in_specs=[pl.BlockSpec(memory_space=pltpu.VMEM)] * 4,
        out_specs=pl.BlockSpec(memory_space=pltpu.VMEM),
        scratch_shapes=scratch(rows),
        name="update",
    )(c, r, p, distances)


def solution(mesh):
    spec = P("row", "col")
    return jax.shard_map(on_device, mesh=mesh, in_specs=(spec,), out_specs=spec, check_vma=False)
```

```python
import functools

import jax
import jax.numpy as jnp
from jax import lax
from jax.experimental import pallas as pl
from jax.experimental.pallas import tpu as pltpu
from jax.sharding import PartitionSpec as P

B = 256
NB = 64
KB = 16
MESH = pl.DeviceIdType.MESH
STEP = ((1, 0), (0, 1), (3, 0), (0, 3))
SENDS = ((0, 4, 5, 6, 8, 9, 10, 11), (4, 5), (5, 6, 7), (4, 8))
DEPTHS = ((0,), (4,), (5, 7, 8), (1, 6, 9, 3, 11, 12), (2, 10, 13, 15), (14,))
TAKES = ((4, 8, 9, 10, 12, 13, 14, 15), (5, 6), (1, 2, 3), (7, 11))
HOP = 3
P_SLOT = 2


def member(value, items):
    return functools.reduce(jnp.logical_or, [value == i for i in items])


def gather_kernel(d_ref, c_ref, r_ref, p_ref, csend, crecv, rsend, rrecv, psend, precv):
    row, z = lax.axis_index("row"), lax.axis_index("col")
    core, chip = row % 2, row // 2
    x, y = chip % 4, chip // 4
    sibling = (row + 1 - 2 * core, z)
    root = row == 0
    plus = z < 4
    minus = jnp.logical_or(z == 0, z > 5)
    up, down = (row, (z + 1) % 8), (row, (z + 7) % 8)
    n, nc = B // NB, c_ref.shape[0] // NB
    width = r_ref.shape[1] // 4

    def number(flag):
        return jnp.where(flag, 1, 0)

    def both(*flags):
        return functools.reduce(jnp.logical_and, flags)

    def chip_at(step, side):
        dx, dy = step
        return (2 * (((y + dy) % 4) * 4 + (x + dx) % 4) + side, z)

    frame = ((x, y), (y, (4 - x) % 4), ((4 - x) % 4, (4 - y) % 4), ((4 - y) % 4, x))
    forks, depth, mine = [], [], []
    barrier = pltpu.get_barrier_semaphore()

    def greet(device):
        pl.semaphore_signal(barrier, inc=1, device_id=device, device_id_type=MESH)

    expected = 1 + number(plus) + number(minus)
    for q in range(4):
        side = q // 2
        place = frame[q][0] * 4 + frame[q][1]
        mine.append(both(chip > 0, core == side))
        carries = jnp.logical_or(root, mine[q])
        forks.append([])
        for d in range(4):
            step = STEP[(d + q) % 4]
            flag = both(carries, member(place, SENDS[d]))
            forks[q].append((flag, chip_at(step, side)))
            expected = expected + number(flag)
            back = (4 - step[0]) % 4, (4 - step[1]) % 4

            @pl.when(both(mine[q], member(place, TAKES[d])))
            def _():
                source, at = chip_at(back, side)
                greet((jnp.where(source < 2, 0, source), at))

        depth.append(sum(number(member(place, DEPTHS[k])) * k for k in range(1, 6)))

    greet(sibling)
    front = core == 0
    expected = expected + number(front) * 15 + number(both(front, z == 0)) * 7

    @pl.when(front)
    def _():
        @pl.loop(1, 16)
        def _(i):
            greet((2 * ((chip + i) % 16), z))

        @pl.when(z > 0)
        def _():
            greet((row, 0))

    @pl.when(both(z > 0, z < 5))
    def _():
        greet(down)

    @pl.when(z > 4)
    def _():
        greet(up)

    pl.semaphore_wait(barrier, expected)

    def remote(src, dst, send_sem, recv_sem, device):
        return pltpu.make_async_remote_copy(
            src_ref=src, dst_ref=dst, send_sem=send_sem, recv_sem=recv_sem, device_id=device, device_id_type=MESH
        )

    def start(flag, copy):
        @pl.when(flag)
        def _():
            copy.start()

    def finish(flag, part, send_sem, recv_sem):
        @pl.when(flag)
        def _():
            remote(part, part, send_sem, recv_sem, sibling).wait_send()

    def await_part(part, send_sem, recv_sem):
        remote(part, part, send_sem, recv_sem, sibling).wait_recv()

    def c_part(i):
        return pl.ds(pl.multiple_of(i * NB, NB), NB), slice(0, B)

    def r_part(q, j):
        return pl.ds(pl.multiple_of(j * NB, NB), NB), slice(q * width, (q + 1) * width)

    piece = B // 16

    def p_part(i):
        return pl.ds(pl.multiple_of(i * piece, piece), piece), slice(0, B)

    @pl.when(both(root, z == 0))
    def _():
        @pl.loop(1, 16)
        def _(i):
            remote(d_ref.at[p_part(i)], p_ref.at[p_part(i)], psend.at[0, i], precv.at[i], (2 * i, 0)).start()

        pltpu.make_async_copy(d_ref.at[p_part(0)], p_ref.at[p_part(0)], precv.at[0]).start()

    @pl.when(z == 0)
    def _():
        @pl.loop(0, nc)
        def _(i):
            pltpu.make_async_copy(d_ref.at[c_part(i)], c_ref.at[c_part(i)], crecv.at[i]).start()

    @pl.when(root)
    def _():
        @pl.loop(0, n)
        def _(j):
            for q in range(4):
                part = r_part(q, j)
                pltpu.make_async_copy(d_ref.at[part], r_ref.at[part], rrecv.at[q, j]).start()

    def take_c(i):
        part = c_ref.at[c_part(i)]
        await_part(part, csend.at[i, 0], crecv.at[i])
        start(plus, remote(part, part, csend.at[i, 0], crecv.at[i], up))
        start(minus, remote(part, part, csend.at[i, 1], crecv.at[i], down))

    def take_r(q, j):
        part = r_ref.at[r_part(q, j)]
        await_part(part, rsend.at[q, j, 0], rrecv.at[q, j])
        for d, (flag, device) in enumerate(forks[q]):
            start(flag, remote(part, part, rsend.at[q, j, d], rrecv.at[q, j], device))
        remote(part, part, rsend.at[q, j, 4], rrecv.at[q, j], sibling).start()

    own = p_ref.at[p_part(chip)]

    def share_piece():
        await_part(own, psend.at[1, 0], precv.at[chip])

        @pl.when(z == 0)
        def _():
            @pl.loop(1, 8)
            def _(i):
                remote(own, own, psend.at[3, i], precv.at[chip], (row, i)).start()

        @pl.loop(1, 16)
        def _(i):
            remote(own, own, psend.at[1, i], precv.at[chip], (2 * ((chip + i) % 16), z)).start()

        remote(own, own, psend.at[2, 0], precv.at[chip], sibling).start()

    def pass_piece(i):
        part = p_ref.at[p_part((chip + i) % 16)]
        await_part(part, psend.at[2, i], precv.at[(chip + i) % 16])
        remote(part, part, psend.at[2, i], precv.at[(chip + i) % 16], sibling).start()

    carrying = [jnp.logical_or(root, mine[q]) for q in range(4)]

    reach = jnp.where(z < 5, z, 8 - z)

    @pl.loop(0, max(5 * HOP + n, 4 * HOP + 3 * nc // 2 + 1))
    def _(t):
        u = t - HOP * reach
        i = (2 * u + u % 3) // 3

        @pl.when(both(front, t == jnp.where(z == 0, 0, P_SLOT)))
        def _():
            share_piece()

        @pl.when(both(u >= 0, u % 3 < 2, i < nc))
        def _():
            take_c(i)

        for q in range(4):
            j = t - HOP * depth[q]

            @pl.when(both(carrying[q], j >= 0, j < n))
            def _():
                take_r(q, j)

    @pl.when(front)
    def _():
        @pl.loop(1, 16)
        def _(i):
            pass_piece(i)

    @pl.loop(0, n)
    def _(j):
        for q in range(4):
            part = r_ref.at[r_part(q, j)]

            @pl.when(jnp.logical_not(carrying[q]))
            def _():
                await_part(part, rsend.at[q, j, 0], rrecv.at[q, j])

            for d in range(4):
                finish(forks[q][d][0], part, rsend.at[q, j, d], rrecv.at[q, j])
            finish(carrying[q], part, rsend.at[q, j, 4], rrecv.at[q, j])

    @pl.loop(0, nc)
    def _(i):
        part = c_ref.at[c_part(i)]
        finish(plus, part, csend.at[i, 0], crecv.at[i])
        finish(minus, part, csend.at[i, 1], crecv.at[i])

    @pl.when(both(front, root, z == 0))
    def _():
        @pl.loop(1, 16)
        def _(i):
            part = p_ref.at[p_part(i)]
            remote(part, part, psend.at[0, i], precv.at[i], sibling).wait_send()

    @pl.when(both(front, z == 0))
    def _():
        @pl.loop(1, 8)
        def _(i):
            remote(own, own, psend.at[3, i], precv.at[chip], sibling).wait_send()

    @pl.when(front)
    def _():
        @pl.loop(1, 16)
        def _(i):
            remote(own, own, psend.at[1, i], precv.at[chip], sibling).wait_send()

        @pl.loop(0, 16)
        def _(i):
            remote(own, own, psend.at[2, i], precv.at[chip], sibling).wait_send()

    @pl.when(jnp.logical_not(front))
    def _():
        @pl.loop(0, 16)
        def _(i):
            part = p_ref.at[p_part(i)]
            await_part(part, psend.at[0, 0], precv.at[i])


def gather(distances):
    rows, cols = distances.shape
    f32 = jnp.float32
    return pl.pallas_call(
        gather_kernel,
        out_shape=(
            jax.ShapeDtypeStruct((rows, B), f32),
            jax.ShapeDtypeStruct((B, cols), f32),
            jax.ShapeDtypeStruct((B, B), f32),
        ),
        in_specs=[pl.BlockSpec(memory_space=pl.ANY)],
        out_specs=[pl.BlockSpec(memory_space=pltpu.VMEM)] * 3,
        scratch_shapes=[
            pltpu.SemaphoreType.DMA((rows // NB, 2)),
            pltpu.SemaphoreType.DMA((rows // NB,)),
            pltpu.SemaphoreType.DMA((4, B // NB, 5)),
            pltpu.SemaphoreType.DMA((4, B // NB)),
            pltpu.SemaphoreType.DMA((4, 16)),
            pltpu.SemaphoreType.DMA((16,)),
        ],
        compiler_params=pltpu.CompilerParams(collective_id=0, has_side_effects=True),
        name="gather",
    )(distances)


def close_and_extend(p_ref, c_ref, z_refs, wide_refs, panel_refs, old_ref, square_ref, hot_ref):
    strips = len(z_refs)
    left_strips = B // 128
    for r in range(0, B, 128):
        for t in range(left_strips):
            z_refs[t][r : r + 128, :] = p_ref[t * 128 : t * 128 + 128, r : r + 128].T
        for t in range(strips - left_strips):
            z_refs[left_strips + t][r : r + 128, :] = c_ref[t * 128 : t * 128 + 128, r : r + 128].T
    rows = lax.broadcasted_iota(jnp.int32, (B, 128), 0) % 128
    for l in range(KB):
        hot_ref[:, l * 128 : l * 128 + 128] = jnp.where(rows == l, 1.0, 0.0).astype(jnp.bfloat16)

    def lanes(t):
        return slice(t * 128, t * 128 + 128)

    def spread(ref, row, t):
        view = ref.at[row // 8 * 8 : row // 8 * 8 + 8, lanes(t)]
        line = view[pl.ds(row % 8, 8, stride=0), :]
        return jnp.concatenate([line] * (KB // 8), 0)

    def block(k):
        return pl.ds(pl.multiple_of(k, KB), KB)

    def turn(value, k):
        return pltpu.roll(value, lax.rem(128 - lax.rem(k, 128), 128), 1)

    def widen(slot, k, first):
        column = turn(z_refs[first][...], k)
        high = jnp.floor(column * (1 / 32)) * 32
        split = jnp.concatenate([high, column - high], 1).astype(jnp.bfloat16)
        for c in range(0, KB * 128, 512):
            wide_refs[slot][:, c : c + 512] = jnp.dot(split, hot_ref[:, c : c + 512], preferred_element_type=jnp.float32)

    def close(slot, k, first, tiles):
        square = turn(old_ref[:, lanes(first)], k)
        for step in range(KB.bit_length() - 1):
            square_ref[step] = square
            left = square[:, :KB]
            for l in range(KB):
                square = jnp.minimum(square, left[:, l : l + 1] + spread(square_ref.at[step], l, 0))
        values = [old_ref[:, lanes(t)] for t in tiles]
        for l in range(KB):
            column = jnp.broadcast_to(square[:, l : l + 1], (KB, 128))
            values = [jnp.minimum(v, column + spread(old_ref, l, t)) for v, t in zip(values, tiles)]
        for v, t in zip(values, tiles):
            panel_refs[slot][:, lanes(t)] = v

    def through(slot, starts, tiles):
        values = [[z_refs[t][block(r), :] for t in tiles] for r in starts]
        for l in range(KB):
            lines = [spread(panel_refs[slot], l, t) for t in tiles]
            for n, r in enumerate(starts):
                column = wide_refs[slot][block(r), lanes(l)]
                values[n] = [jnp.minimum(v, column + line) for v, line in zip(values[n], lines)]
        return values

    def update(slot, starts, tiles):
        for r, row in zip(starts, through(slot, starts, tiles)):
            for t, value in zip(tiles, row):
                z_refs[t][block(r), :] = value

    right = list(range(left_strips, strips))

    def stage(slot, k, first, others):
        after = k + KB
        rest = [lax.rem(after + r, B) for r in range(KB, B - KB, KB)]
        live = [first] + others
        for t, value in zip(live, through(slot, [after], live)[0]):
            old_ref[:, lanes(t)] = value
        update(slot, rest, [first])
        close(1 - slot, after, first, live)
        widen(1 - slot, after, first)
        for r in rest:
            update(slot, [r], others)
        for t in live:
            z_refs[t][block(after), :] = panel_refs[1 - slot][:, lanes(t)]

    def pair(start, first, others):
        def run(i, carry):
            k = start + i * (2 * KB)
            stage(1, k, first, others)
            stage(0, k + KB, first, others)
            return carry

        return run

    widen(0, 0, 0)
    for t in range(strips):
        old_ref[:, lanes(t)] = z_refs[t][0:KB, :]
    close(0, 0, 0, list(range(strips)))
    for t in range(strips):
        z_refs[t][0:KB, :] = panel_refs[0][:, lanes(t)]
    stage(0, 0, 0, [1] + right)
    lax.fori_loop(0, 3, pair(KB, 0, [1] + right), 0)
    lax.fori_loop(0, 4, pair(128 - KB, 1, right), 0)
    for r in range(0, B - KB, KB):
        update(1, [r], right)
    for t in range(strips - left_strips):
        for r in range(0, B, 128):
            c_ref[t * 128 : t * 128 + 128, r : r + 128] = z_refs[left_strips + t][r : r + 128, :].T


TI, TJ, U = 24, 512, 32


def min_plus(x_ref, y_ref, acc_ref, wide_ref, finished):
    height, depth = x_ref.shape
    breadth = y_ref.shape[1]
    blocks, strips = height // TI, breadth // TJ
    share = 8 * (-(-(TI // 8) // strips))

    def widen(slot, left, row0, l0):
        for u in range(U):
            wide_ref[slot, l0 + u, row0 : row0 + share, :] = jnp.broadcast_to(left[:, u : u + 1], (share, 128))
        return pltpu.roll(left, 128 - U, 1)

    for s in range(TI // share):
        for half in range(depth // 128):

            def first(g, left):
                return widen(0, left, s * share, pl.multiple_of(half * 128 + g * U, U))

            lax.fori_loop(0, 128 // U, first, x_ref[s * share : (s + 1) * share, half * 128 : half * 128 + 128])

    def block(b, carry):
        slot = lax.rem(b, 2)
        row0 = pl.multiple_of(b * TI, TI)
        next0 = pl.multiple_of(jnp.minimum(b + 1, blocks - 1) * TI, TI)
        for s in range(strips):
            strip = slice(s * TJ, (s + 1) * TJ)
            value = acc_ref[pl.ds(row0, TI), strip]
            for half in range(depth // 128):

                def group(g, state):
                    value, left = state
                    l0 = pl.multiple_of(half * 128 + g * U, U)
                    right = y_ref.at[pl.ds(l0, U), strip]
                    for u in range(U):
                        wide = wide_ref[slot, l0 + u]
                        row = right[pl.ds(u, 8, stride=0), :]
                        value = jnp.concatenate(
                            [
                                jnp.minimum(
                                    value[:, c : c + 128], wide + jnp.concatenate([row[:, c : c + 128]] * (TI // 8), 0)
                                )
                                for c in range(0, TJ, 128)
                            ],
                            1,
                        )
                    if s * share < TI:
                        left = widen(1 - slot, left, s * share, l0)
                    return value, left

                left = x_ref[pl.ds(next0 + s * share, share), half * 128 : half * 128 + 128]
                value, left = lax.fori_loop(0, 128 // U, group, (value, left))
            acc_ref[pl.ds(row0, TI), strip] = value
        finished(pl.ds(row0, TI), b)
        return carry

    lax.fori_loop(0, blocks, block, 0)


def update_kernel(
    c_ref, p_ref, r_hbm, d_hbm, out_hbm, x_ref, old_ref, square_ref, hot_ref, wide_ref, r_ref, d_ref, sem, out_sem, *more
):
    r_copy = pltpu.make_async_copy(r_hbm, r_ref, sem.at[0])
    d_copy = pltpu.make_async_copy(d_hbm, d_ref, sem.at[1])
    r_copy.start()
    d_copy.start()
    x_ref[...] = c_ref[...]
    close_and_extend(p_ref, x_ref, more[4:], more[:2], more[2:4], old_ref, square_ref, hot_ref)
    r_copy.wait()
    d_copy.wait()

    def put(rows, b):
        return pltpu.make_async_copy(d_ref.at[rows, :], out_hbm.at[rows, :], out_sem.at[b])

    min_plus(x_ref, r_ref, d_ref, wide_ref, lambda rows, b: put(rows, b).start())

    @pl.loop(0, d_ref.shape[0] // TI)
    def _(b):
        put(pl.ds(pl.multiple_of(b * TI, TI), TI), b).wait()


def scratch(rows, cols):
    f32 = jnp.float32
    width = B + rows
    return [
        pltpu.VMEM((rows, B), f32),
        pltpu.VMEM((KB, width), f32),
        pltpu.VMEM((KB.bit_length(), KB, 128), f32),
        pltpu.VMEM((B, KB * 128), jnp.bfloat16),
        pltpu.VMEM((2, B, TI, 128), f32),
        pltpu.VMEM((B, cols), f32),
        pltpu.VMEM((rows, cols), f32),
        pltpu.SemaphoreType.DMA((2,)),
        pltpu.SemaphoreType.DMA((rows // TI,)),
        *[pltpu.VMEM((B, KB * 128), f32)] * 2,
        *[pltpu.VMEM((KB, width), f32)] * 2,
        *[pltpu.VMEM((B, 128), f32)] * (width // 128),
    ]


def on_device(distances):
    rows, cols = distances.shape
    f32 = jnp.float32
    c, r, p = gather(distances)
    return pl.pallas_call(
        update_kernel,
        out_shape=jax.ShapeDtypeStruct((rows, cols), f32),
        in_specs=[pl.BlockSpec(memory_space=pltpu.VMEM)] * 2 + [pl.BlockSpec(memory_space=pl.ANY)] * 2,
        out_specs=pl.BlockSpec(memory_space=pl.ANY),
        scratch_shapes=scratch(rows, cols),
        name="update",
    )(c, p, r, distances)


def solution(mesh):
    spec = P("row", "col")
    return jax.shard_map(on_device, mesh=mesh, in_specs=(spec,), out_specs=spec, check_vma=False)
```

```python
import functools

import jax
import jax.numpy as jnp
from jax import lax
from jax.experimental import pallas as pl
from jax.experimental.pallas import tpu as pltpu
from jax.sharding import PartitionSpec as P

B = 256
NB = 64
KB = 16
MESH = pl.DeviceIdType.MESH
STEP = ((1, 0), (0, 1), (3, 0), (0, 3))
SENDS = ((0, 4, 5, 6, 8, 9, 10, 11), (4, 5), (5, 6, 7), (4, 8))
DEPTHS = ((0,), (4,), (5, 7, 8), (1, 6, 9, 3, 11, 12), (2, 10, 13, 15), (14,))
TAKES = ((4, 8, 9, 10, 12, 13, 14, 15), (5, 6), (1, 2, 3), (7, 11))
HOP = 3
P_SLOT = 2


def member(value, items):
    return functools.reduce(jnp.logical_or, [value == i for i in items])


def gather_kernel(d_ref, c_ref, r_ref, p_ref, csend, crecv, rsend, rrecv, psend, precv):
    row, z = lax.axis_index("row"), lax.axis_index("col")
    core, chip = row % 2, row // 2
    x, y = chip % 4, chip // 4
    sibling = (row + 1 - 2 * core, z)
    root = row == 0
    plus = z < 4
    minus = jnp.logical_or(z == 0, z > 5)
    up, down = (row, (z + 1) % 8), (row, (z + 7) % 8)
    n, nc = B // NB, c_ref.shape[0] // NB
    width = r_ref.shape[1] // 4

    def number(flag):
        return jnp.where(flag, 1, 0)

    def both(*flags):
        return functools.reduce(jnp.logical_and, flags)

    def chip_at(step, side):
        dx, dy = step
        return (2 * (((y + dy) % 4) * 4 + (x + dx) % 4) + side, z)

    frame = ((x, y), (y, (4 - x) % 4), ((4 - x) % 4, (4 - y) % 4), ((4 - y) % 4, x))
    forks, depth, mine = [], [], []
    barrier = pltpu.get_barrier_semaphore()

    def greet(device):
        pl.semaphore_signal(barrier, inc=1, device_id=device, device_id_type=MESH)

    expected = 1 + number(plus) + number(minus)
    for q in range(4):
        side = q // 2
        place = frame[q][0] * 4 + frame[q][1]
        mine.append(both(chip > 0, core == side))
        carries = jnp.logical_or(root, mine[q])
        forks.append([])
        for d in range(4):
            step = STEP[(d + q) % 4]
            flag = both(carries, member(place, SENDS[d]))
            forks[q].append((flag, chip_at(step, side)))
            expected = expected + number(flag)
            back = (4 - step[0]) % 4, (4 - step[1]) % 4

            @pl.when(both(mine[q], member(place, TAKES[d])))
            def _():
                source, at = chip_at(back, side)
                greet((jnp.where(source < 2, 0, source), at))

        depth.append(sum(number(member(place, DEPTHS[k])) * k for k in range(1, 6)))

    greet(sibling)
    front = core == 0
    expected = expected + number(front) * 15 + number(both(front, z == 0)) * 7

    @pl.when(front)
    def _():
        @pl.loop(1, 16)
        def _(i):
            greet((2 * ((chip + i) % 16), z))

        @pl.when(z > 0)
        def _():
            greet((row, 0))

    @pl.when(both(z > 0, z < 5))
    def _():
        greet(down)

    @pl.when(z > 4)
    def _():
        greet(up)

    pl.semaphore_wait(barrier, expected)

    def remote(src, dst, send_sem, recv_sem, device):
        return pltpu.make_async_remote_copy(
            src_ref=src, dst_ref=dst, send_sem=send_sem, recv_sem=recv_sem, device_id=device, device_id_type=MESH
        )

    def start(flag, copy):
        @pl.when(flag)
        def _():
            copy.start()

    def finish(flag, part, send_sem, recv_sem):
        @pl.when(flag)
        def _():
            remote(part, part, send_sem, recv_sem, sibling).wait_send()

    def await_part(part, send_sem, recv_sem):
        remote(part, part, send_sem, recv_sem, sibling).wait_recv()

    def c_part(i):
        return pl.ds(pl.multiple_of(i * NB, NB), NB), slice(0, B)

    def r_part(q, j):
        return pl.ds(pl.multiple_of(j * NB, NB), NB), slice(q * width, (q + 1) * width)

    piece = B // 16

    def p_part(i):
        return pl.ds(pl.multiple_of(i * piece, piece), piece), slice(0, B)

    @pl.when(both(root, z == 0))
    def _():
        @pl.loop(1, 16)
        def _(i):
            remote(d_ref.at[p_part(i)], p_ref.at[p_part(i)], psend.at[0, i], precv.at[i], (2 * i, 0)).start()

        pltpu.make_async_copy(d_ref.at[p_part(0)], p_ref.at[p_part(0)], precv.at[0]).start()

    @pl.when(z == 0)
    def _():
        @pl.loop(0, nc)
        def _(i):
            pltpu.make_async_copy(d_ref.at[c_part(i)], c_ref.at[c_part(i)], crecv.at[i]).start()

    @pl.when(root)
    def _():
        @pl.loop(0, n)
        def _(j):
            for q in range(4):
                part = r_part(q, j)
                pltpu.make_async_copy(d_ref.at[part], r_ref.at[part], rrecv.at[q, j]).start()

    def take_c(i):
        part = c_ref.at[c_part(i)]
        await_part(part, csend.at[i, 0], crecv.at[i])
        start(plus, remote(part, part, csend.at[i, 0], crecv.at[i], up))
        start(minus, remote(part, part, csend.at[i, 1], crecv.at[i], down))

    def take_r(q, j):
        part = r_ref.at[r_part(q, j)]
        await_part(part, rsend.at[q, j, 0], rrecv.at[q, j])
        for d, (flag, device) in enumerate(forks[q]):
            start(flag, remote(part, part, rsend.at[q, j, d], rrecv.at[q, j], device))
        remote(part, part, rsend.at[q, j, 4], rrecv.at[q, j], sibling).start()

    own = p_ref.at[p_part(chip)]

    def share_piece():
        await_part(own, psend.at[1, 0], precv.at[chip])

        @pl.when(z == 0)
        def _():
            @pl.loop(1, 8)
            def _(i):
                remote(own, own, psend.at[3, i], precv.at[chip], (row, i)).start()

        @pl.loop(1, 16)
        def _(i):
            remote(own, own, psend.at[1, i], precv.at[chip], (2 * ((chip + i) % 16), z)).start()

        remote(own, own, psend.at[2, 0], precv.at[chip], sibling).start()

    def pass_piece(i):
        part = p_ref.at[p_part((chip + i) % 16)]
        await_part(part, psend.at[2, i], precv.at[(chip + i) % 16])
        remote(part, part, psend.at[2, i], precv.at[(chip + i) % 16], sibling).start()

    carrying = [jnp.logical_or(root, mine[q]) for q in range(4)]

    reach = jnp.where(z < 5, z, 8 - z)

    @pl.loop(0, max(5 * HOP + n, 4 * HOP + 3 * nc // 2 + 1))
    def _(t):
        u = t - HOP * reach
        i = (2 * u + u % 3) // 3

        @pl.when(both(front, t == jnp.where(z == 0, 0, P_SLOT)))
        def _():
            share_piece()

        @pl.when(both(u >= 0, u % 3 < 2, i < nc))
        def _():
            take_c(i)

        for q in range(4):
            j = t - HOP * depth[q]

            @pl.when(both(carrying[q], j >= 0, j < n))
            def _():
                take_r(q, j)

    @pl.when(front)
    def _():
        @pl.loop(1, 16)
        def _(i):
            pass_piece(i)

    @pl.loop(0, n)
    def _(j):
        for q in range(4):
            part = r_ref.at[r_part(q, j)]

            @pl.when(jnp.logical_not(carrying[q]))
            def _():
                await_part(part, rsend.at[q, j, 0], rrecv.at[q, j])

            for d in range(4):
                finish(forks[q][d][0], part, rsend.at[q, j, d], rrecv.at[q, j])
            finish(carrying[q], part, rsend.at[q, j, 4], rrecv.at[q, j])

    @pl.loop(0, nc)
    def _(i):
        part = c_ref.at[c_part(i)]
        finish(plus, part, csend.at[i, 0], crecv.at[i])
        finish(minus, part, csend.at[i, 1], crecv.at[i])

    @pl.when(both(front, root, z == 0))
    def _():
        @pl.loop(1, 16)
        def _(i):
            part = p_ref.at[p_part(i)]
            remote(part, part, psend.at[0, i], precv.at[i], sibling).wait_send()

    @pl.when(both(front, z == 0))
    def _():
        @pl.loop(1, 8)
        def _(i):
            remote(own, own, psend.at[3, i], precv.at[chip], sibling).wait_send()

    @pl.when(front)
    def _():
        @pl.loop(1, 16)
        def _(i):
            remote(own, own, psend.at[1, i], precv.at[chip], sibling).wait_send()

        @pl.loop(0, 16)
        def _(i):
            remote(own, own, psend.at[2, i], precv.at[chip], sibling).wait_send()

    @pl.when(jnp.logical_not(front))
    def _():
        @pl.loop(0, 16)
        def _(i):
            part = p_ref.at[p_part(i)]
            await_part(part, psend.at[0, 0], precv.at[i])


def gather(distances):
    rows, cols = distances.shape
    f32 = jnp.float32
    return pl.pallas_call(
        gather_kernel,
        out_shape=(
            jax.ShapeDtypeStruct((rows, B), f32),
            jax.ShapeDtypeStruct((B, cols), f32),
            jax.ShapeDtypeStruct((B, B), f32),
        ),
        in_specs=[pl.BlockSpec(memory_space=pl.ANY)],
        out_specs=[pl.BlockSpec(memory_space=pltpu.VMEM)] * 3,
        scratch_shapes=[
            pltpu.SemaphoreType.DMA((rows // NB, 2)),
            pltpu.SemaphoreType.DMA((rows // NB,)),
            pltpu.SemaphoreType.DMA((4, B // NB, 5)),
            pltpu.SemaphoreType.DMA((4, B // NB)),
            pltpu.SemaphoreType.DMA((4, 16)),
            pltpu.SemaphoreType.DMA((16,)),
        ],
        compiler_params=pltpu.CompilerParams(collective_id=0, has_side_effects=True),
        name="gather",
    )(distances)


def close_and_extend(p_ref, c_ref, z_refs, wide_refs, panel_refs, old_ref, square_ref, hot_ref):
    strips = len(z_refs)
    left_strips = B // 128
    for r in range(0, B, 128):
        for t in range(left_strips):
            z_refs[t][r : r + 128, :] = p_ref[t * 128 : t * 128 + 128, r : r + 128].T
        for t in range(strips - left_strips):
            z_refs[left_strips + t][r : r + 128, :] = c_ref[t * 128 : t * 128 + 128, r : r + 128].T
    rows = lax.broadcasted_iota(jnp.int32, (B, 128), 0) % 128
    for l in range(KB):
        hot_ref[:, l * 128 : l * 128 + 128] = jnp.where(rows == l, 1.0, 0.0).astype(jnp.bfloat16)

    def lanes(t):
        return slice(t * 128, t * 128 + 128)

    def spread(ref, row, t):
        view = ref.at[row // 8 * 8 : row // 8 * 8 + 8, lanes(t)]
        line = view[pl.ds(row % 8, 8, stride=0), :]
        return jnp.concatenate([line] * (KB // 8), 0)

    def block(k):
        return pl.ds(pl.multiple_of(k, KB), KB)

    def turn(value, k):
        return pltpu.roll(value, lax.rem(128 - lax.rem(k, 128), 128), 1)

    def widen(slot, k, first):
        column = turn(z_refs[first][...], k)
        high = jnp.floor(column * (1 / 32)) * 32
        split = jnp.concatenate([high, column - high], 1).astype(jnp.bfloat16)
        for c in range(0, KB * 128, 512):
            wide_refs[slot][:, c : c + 512] = jnp.dot(split, hot_ref[:, c : c + 512], preferred_element_type=jnp.float32)

    def close(slot, k, first, tiles, beside=None):
        square = turn(old_ref[:, lanes(first)], k)
        for step in range(KB.bit_length() - 1):
            square_ref[step] = square
            left = square[:, :KB]
            for l in range(KB):
                square = jnp.minimum(square, left[:, l : l + 1] + spread(square_ref.at[step], l, 0))
            if beside is not None:
                square = jnp.minimum(square, beside(step) + 8192.0)
        values = [old_ref[:, lanes(t)] for t in tiles]
        for l in range(KB):
            column = jnp.broadcast_to(square[:, l : l + 1], (KB, 128))
            values = [jnp.minimum(v, column + spread(old_ref, l, t)) for v, t in zip(values, tiles)]
        for v, t in zip(values, tiles):
            panel_refs[slot][:, lanes(t)] = v

    def through(slot, starts, tiles):
        values = [[z_refs[t][block(r), :] for t in tiles] for r in starts]
        for l in range(KB):
            lines = [spread(panel_refs[slot], l, t) for t in tiles]
            for n, r in enumerate(starts):
                column = wide_refs[slot][block(r), lanes(l)]
                values[n] = [jnp.minimum(v, column + line) for v, line in zip(values[n], lines)]
        return values

    def update(slot, starts, tiles):
        for r, row in zip(starts, through(slot, starts, tiles)):
            for t, value in zip(tiles, row):
                z_refs[t][block(r), :] = value
        return value

    right = list(range(left_strips, strips))

    def stage(slot, k, first, others):
        after = k + KB
        rest = [lax.rem(after + r, B) for r in range(KB, B - KB, KB)]
        live = [first] + others
        for t, value in zip(live, through(slot, [after], live)[0]):
            old_ref[:, lanes(t)] = value
        update(slot, rest, [first])

        def beside(step):
            tokens = [update(slot, [r], others) for r in rest[3 * step : 3 * step + 3]]
            return functools.reduce(jnp.minimum, tokens)

        widen(1 - slot, after, first)
        close(1 - slot, after, first, live, beside)
        for r in rest[3 * (KB.bit_length() - 1) :]:
            update(slot, [r], others)
        for t in live:
            z_refs[t][block(after), :] = panel_refs[1 - slot][:, lanes(t)]

    def pair(start, first, others):
        def run(i, carry):
            k = start + i * (2 * KB)
            stage(1, k, first, others)
            stage(0, k + KB, first, others)
            return carry

        return run

    widen(0, 0, 0)
    for t in range(strips):
        old_ref[:, lanes(t)] = z_refs[t][0:KB, :]
    close(0, 0, 0, list(range(strips)))
    for t in range(strips):
        z_refs[t][0:KB, :] = panel_refs[0][:, lanes(t)]
    stage(0, 0, 0, [1] + right)
    lax.fori_loop(0, 3, pair(KB, 0, [1] + right), 0)
    lax.fori_loop(0, 4, pair(128 - KB, 1, right), 0)
    for r in range(0, B - KB, KB):
        update(1, [r], right)
    for t in range(strips - left_strips):
        for r in range(0, B, 128):
            c_ref[t * 128 : t * 128 + 128, r : r + 128] = z_refs[left_strips + t][r : r + 128, :].T


TI, TJ, U = 24, 512, 32


def min_plus(x_ref, y_ref, acc_ref, wide_ref, finished):
    height, depth = x_ref.shape
    breadth = y_ref.shape[1]
    blocks, strips = height // TI, breadth // TJ
    share = 8 * (-(-(TI // 8) // strips))

    def widen(slot, left, row0, l0):
        for u in range(U):
            wide_ref[slot, l0 + u, row0 : row0 + share, :] = jnp.broadcast_to(left[:, u : u + 1], (share, 128))
        return pltpu.roll(left, 128 - U, 1)

    for s in range(TI // share):
        for half in range(depth // 128):

            def first(g, left):
                return widen(0, left, s * share, pl.multiple_of(half * 128 + g * U, U))

            lax.fori_loop(0, 128 // U, first, x_ref[s * share : (s + 1) * share, half * 128 : half * 128 + 128])

    def block(b, carry):
        slot = lax.rem(b, 2)
        row0 = pl.multiple_of(b * TI, TI)
        next0 = pl.multiple_of(jnp.minimum(b + 1, blocks - 1) * TI, TI)
        for s in range(strips):
            strip = slice(s * TJ, (s + 1) * TJ)
            value = acc_ref[pl.ds(row0, TI), strip]
            for half in range(depth // 128):

                def group(g, state):
                    value, left = state
                    l0 = pl.multiple_of(half * 128 + g * U, U)
                    right = y_ref.at[pl.ds(l0, U), strip]
                    for u in range(U):
                        wide = wide_ref[slot, l0 + u]
                        row = right[pl.ds(u, 8, stride=0), :]
                        value = jnp.concatenate(
                            [
                                jnp.minimum(
                                    value[:, c : c + 128], wide + jnp.concatenate([row[:, c : c + 128]] * (TI // 8), 0)
                                )
                                for c in range(0, TJ, 128)
                            ],
                            1,
                        )
                    if s * share < TI:
                        left = widen(1 - slot, left, s * share, l0)
                    return value, left

                left = x_ref[pl.ds(next0 + s * share, share), half * 128 : half * 128 + 128]
                value, left = lax.fori_loop(0, 128 // U, group, (value, left))
            acc_ref[pl.ds(row0, TI), strip] = value
        finished(pl.ds(row0, TI), b)
        return carry

    lax.fori_loop(0, blocks, block, 0)


def update_kernel(
    c_ref, p_ref, r_hbm, d_hbm, out_hbm, x_ref, old_ref, square_ref, hot_ref, wide_ref, r_ref, d_ref, sem, out_sem, *more
):
    r_copy = pltpu.make_async_copy(r_hbm, r_ref, sem.at[0])
    d_copy = pltpu.make_async_copy(d_hbm, d_ref, sem.at[1])
    r_copy.start()
    d_copy.start()
    x_ref[...] = c_ref[...]
    close_and_extend(p_ref, x_ref, more[4:], more[:2], more[2:4], old_ref, square_ref, hot_ref)
    r_copy.wait()
    d_copy.wait()

    def put(rows, b):
        return pltpu.make_async_copy(d_ref.at[rows, :], out_hbm.at[rows, :], out_sem.at[b])

    min_plus(x_ref, r_ref, d_ref, wide_ref, lambda rows, b: put(rows, b).start())

    @pl.loop(0, d_ref.shape[0] // TI)
    def _(b):
        put(pl.ds(pl.multiple_of(b * TI, TI), TI), b).wait()


def scratch(rows, cols):
    f32 = jnp.float32
    width = B + rows
    return [
        pltpu.VMEM((rows, B), f32),
        pltpu.VMEM((KB, width), f32),
        pltpu.VMEM((KB.bit_length(), KB, 128), f32),
        pltpu.VMEM((B, KB * 128), jnp.bfloat16),
        pltpu.VMEM((2, B, TI, 128), f32),
        pltpu.VMEM((B, cols), f32),
        pltpu.VMEM((rows, cols), f32),
        pltpu.SemaphoreType.DMA((2,)),
        pltpu.SemaphoreType.DMA((rows // TI,)),
        *[pltpu.VMEM((B, KB * 128), f32)] * 2,
        *[pltpu.VMEM((KB, width), f32)] * 2,
        *[pltpu.VMEM((B, 128), f32)] * (width // 128),
    ]


def on_device(distances):
    rows, cols = distances.shape
    f32 = jnp.float32
    c, r, p = gather(distances)
    return pl.pallas_call(
        update_kernel,
        out_shape=jax.ShapeDtypeStruct((rows, cols), f32),
        in_specs=[pl.BlockSpec(memory_space=pltpu.VMEM)] * 2 + [pl.BlockSpec(memory_space=pl.ANY)] * 2,
        out_specs=pl.BlockSpec(memory_space=pl.ANY),
        scratch_shapes=scratch(rows, cols),
        name="update",
    )(c, p, r, distances)


def solution(mesh):
    spec = P("row", "col")
    return jax.shard_map(on_device, mesh=mesh, in_specs=(spec,), out_specs=spec, check_vma=False)
```

```python
import functools

import jax
import jax.numpy as jnp
from jax import lax
from jax.experimental import pallas as pl
from jax.experimental.pallas import tpu as pltpu
from jax.sharding import PartitionSpec as P

B = 256
NB = 64
KB = 16
MESH = pl.DeviceIdType.MESH
STEP = ((1, 0), (0, 1), (3, 0), (0, 3))
SENDS = ((0, 4, 5, 6, 8, 9, 10, 11), (4, 5), (5, 6, 7), (4, 8))
DEPTHS = ((0,), (4,), (5, 7, 8), (1, 6, 9, 3, 11, 12), (2, 10, 13, 15), (14,))
TAKES = ((4, 8, 9, 10, 12, 13, 14, 15), (5, 6), (1, 2, 3), (7, 11))
HOP = 3
P_SLOT = 2


def member(value, items):
    return functools.reduce(jnp.logical_or, [value == i for i in items])


def gather_kernel(d_ref, c_ref, r_ref, p_ref, csend, crecv, rsend, rrecv, psend, precv):
    row, z = lax.axis_index("row"), lax.axis_index("col")
    core, chip = row % 2, row // 2
    x, y = chip % 4, chip // 4
    sibling = (row + 1 - 2 * core, z)
    root = row == 0
    plus = z < 4
    minus = jnp.logical_or(z == 0, z > 5)
    up, down = (row, (z + 1) % 8), (row, (z + 7) % 8)
    n, nc = B // NB, c_ref.shape[0] // NB
    width = r_ref.shape[1] // 4

    def number(flag):
        return jnp.where(flag, 1, 0)

    def both(*flags):
        return functools.reduce(jnp.logical_and, flags)

    def chip_at(step, side):
        dx, dy = step
        return (2 * (((y + dy) % 4) * 4 + (x + dx) % 4) + side, z)

    frame = ((x, y), (y, (4 - x) % 4), ((4 - x) % 4, (4 - y) % 4), ((4 - y) % 4, x))
    forks, depth, mine = [], [], []
    barrier = pltpu.get_barrier_semaphore()

    def greet(device):
        pl.semaphore_signal(barrier, inc=1, device_id=device, device_id_type=MESH)

    expected = 1 + number(plus) + number(minus)
    for q in range(4):
        side = q // 2
        place = frame[q][0] * 4 + frame[q][1]
        mine.append(both(chip > 0, core == side))
        carries = jnp.logical_or(root, mine[q])
        forks.append([])
        for d in range(4):
            step = STEP[(d + q) % 4]
            flag = both(carries, member(place, SENDS[d]))
            forks[q].append((flag, chip_at(step, side)))
            expected = expected + number(flag)
            back = (4 - step[0]) % 4, (4 - step[1]) % 4

            @pl.when(both(mine[q], member(place, TAKES[d])))
            def _():
                source, at = chip_at(back, side)
                greet((jnp.where(source < 2, 0, source), at))

        depth.append(sum(number(member(place, DEPTHS[k])) * k for k in range(1, 6)))

    greet(sibling)
    front = core == 0
    expected = expected + number(front) * 15 + number(both(front, z == 0)) * 7

    @pl.when(front)
    def _():
        @pl.loop(1, 16)
        def _(i):
            greet((2 * ((chip + i) % 16), z))

        @pl.when(z > 0)
        def _():
            greet((row, 0))

    @pl.when(both(z > 0, z < 5))
    def _():
        greet(down)

    @pl.when(z > 4)
    def _():
        greet(up)

    pl.semaphore_wait(barrier, expected)

    def remote(src, dst, send_sem, recv_sem, device):
        return pltpu.make_async_remote_copy(
            src_ref=src, dst_ref=dst, send_sem=send_sem, recv_sem=recv_sem, device_id=device, device_id_type=MESH
        )

    def start(flag, copy):
        @pl.when(flag)
        def _():
            copy.start()

    def finish(flag, part, send_sem, recv_sem):
        @pl.when(flag)
        def _():
            remote(part, part, send_sem, recv_sem, sibling).wait_send()

    def await_part(part, send_sem, recv_sem):
        remote(part, part, send_sem, recv_sem, sibling).wait_recv()

    def c_part(i):
        return pl.ds(pl.multiple_of(i * NB, NB), NB), slice(0, B)

    def r_part(q, j):
        return pl.ds(pl.multiple_of(j * NB, NB), NB), slice(q * width, (q + 1) * width)

    piece = B // 16

    def p_part(i):
        return pl.ds(pl.multiple_of(i * piece, piece), piece), slice(0, B)

    @pl.when(both(root, z == 0))
    def _():
        @pl.loop(1, 16)
        def _(i):
            remote(d_ref.at[p_part(i)], p_ref.at[p_part(i)], psend.at[0, i], precv.at[i], (2 * i, 0)).start()

        pltpu.make_async_copy(d_ref.at[p_part(0)], p_ref.at[p_part(0)], precv.at[0]).start()

    @pl.when(z == 0)
    def _():
        @pl.loop(0, nc)
        def _(i):
            pltpu.make_async_copy(d_ref.at[c_part(i)], c_ref.at[c_part(i)], crecv.at[i]).start()

    @pl.when(root)
    def _():
        @pl.loop(0, n)
        def _(j):
            for q in range(4):
                part = r_part(q, j)
                pltpu.make_async_copy(d_ref.at[part], r_ref.at[part], rrecv.at[q, j]).start()

    def take_c(i):
        part = c_ref.at[c_part(i)]
        await_part(part, csend.at[i, 0], crecv.at[i])
        start(plus, remote(part, part, csend.at[i, 0], crecv.at[i], up))
        start(minus, remote(part, part, csend.at[i, 1], crecv.at[i], down))

    def take_r(q, j):
        part = r_ref.at[r_part(q, j)]
        await_part(part, rsend.at[q, j, 0], rrecv.at[q, j])
        for d, (flag, device) in enumerate(forks[q]):
            start(flag, remote(part, part, rsend.at[q, j, d], rrecv.at[q, j], device))
        remote(part, part, rsend.at[q, j, 4], rrecv.at[q, j], sibling).start()

    own = p_ref.at[p_part(chip)]

    def share_piece():
        await_part(own, psend.at[1, 0], precv.at[chip])

        @pl.when(z == 0)
        def _():
            @pl.loop(1, 8)
            def _(i):
                remote(own, own, psend.at[3, i], precv.at[chip], (row, i)).start()

        @pl.loop(1, 16)
        def _(i):
            remote(own, own, psend.at[1, i], precv.at[chip], (2 * ((chip + i) % 16), z)).start()

        remote(own, own, psend.at[2, 0], precv.at[chip], sibling).start()

    def pass_piece(i):
        part = p_ref.at[p_part((chip + i) % 16)]
        await_part(part, psend.at[2, i], precv.at[(chip + i) % 16])
        remote(part, part, psend.at[2, i], precv.at[(chip + i) % 16], sibling).start()

    carrying = [jnp.logical_or(root, mine[q]) for q in range(4)]

    reach = jnp.where(z < 5, z, 8 - z)

    @pl.loop(0, max(5 * HOP + n, 4 * HOP + 3 * nc // 2 + 1))
    def _(t):
        u = t - HOP * reach
        i = (2 * u + u % 3) // 3

        @pl.when(both(front, t == jnp.where(z == 0, 0, P_SLOT)))
        def _():
            share_piece()

        @pl.when(both(u >= 0, u % 3 < 2, i < nc))
        def _():
            take_c(i)

        for q in range(4):
            j = t - HOP * depth[q]

            @pl.when(both(carrying[q], j >= 0, j < n))
            def _():
                take_r(q, j)

    @pl.when(front)
    def _():
        @pl.loop(1, 16)
        def _(i):
            pass_piece(i)

    @pl.loop(0, n)
    def _(j):
        for q in range(4):
            part = r_ref.at[r_part(q, j)]

            @pl.when(jnp.logical_not(carrying[q]))
            def _():
                await_part(part, rsend.at[q, j, 0], rrecv.at[q, j])

            for d in range(4):
                finish(forks[q][d][0], part, rsend.at[q, j, d], rrecv.at[q, j])
            finish(carrying[q], part, rsend.at[q, j, 4], rrecv.at[q, j])

    @pl.loop(0, nc)
    def _(i):
        part = c_ref.at[c_part(i)]
        finish(plus, part, csend.at[i, 0], crecv.at[i])
        finish(minus, part, csend.at[i, 1], crecv.at[i])

    @pl.when(both(front, root, z == 0))
    def _():
        @pl.loop(1, 16)
        def _(i):
            part = p_ref.at[p_part(i)]
            remote(part, part, psend.at[0, i], precv.at[i], sibling).wait_send()

    @pl.when(both(front, z == 0))
    def _():
        @pl.loop(1, 8)
        def _(i):
            remote(own, own, psend.at[3, i], precv.at[chip], sibling).wait_send()

    @pl.when(front)
    def _():
        @pl.loop(1, 16)
        def _(i):
            remote(own, own, psend.at[1, i], precv.at[chip], sibling).wait_send()

        @pl.loop(0, 16)
        def _(i):
            remote(own, own, psend.at[2, i], precv.at[chip], sibling).wait_send()

    @pl.when(jnp.logical_not(front))
    def _():
        @pl.loop(0, 16)
        def _(i):
            part = p_ref.at[p_part(i)]
            await_part(part, psend.at[0, 0], precv.at[i])


def gather(distances):
    rows, cols = distances.shape
    f32 = jnp.float32
    return pl.pallas_call(
        gather_kernel,
        out_shape=(
            jax.ShapeDtypeStruct((rows, B), f32),
            jax.ShapeDtypeStruct((B, cols), f32),
            jax.ShapeDtypeStruct((B, B), f32),
        ),
        in_specs=[pl.BlockSpec(memory_space=pl.ANY)],
        out_specs=[pl.BlockSpec(memory_space=pltpu.VMEM)] * 3,
        scratch_shapes=[
            pltpu.SemaphoreType.DMA((rows // NB, 2)),
            pltpu.SemaphoreType.DMA((rows // NB,)),
            pltpu.SemaphoreType.DMA((4, B // NB, 5)),
            pltpu.SemaphoreType.DMA((4, B // NB)),
            pltpu.SemaphoreType.DMA((4, 16)),
            pltpu.SemaphoreType.DMA((16,)),
        ],
        compiler_params=pltpu.CompilerParams(collective_id=0, has_side_effects=True),
        name="gather",
    )(distances)


def close_and_extend(p_ref, c_ref, z_refs, wide_refs, panel_refs, old_ref, square_ref, hot_ref):
    strips = len(z_refs)
    left_strips = B // 128
    for r in range(0, B, 128):
        for t in range(left_strips):
            z_refs[t][r : r + 128, :] = p_ref[t * 128 : t * 128 + 128, r : r + 128].T
        for t in range(strips - left_strips):
            z_refs[left_strips + t][r : r + 128, :] = c_ref[t * 128 : t * 128 + 128, r : r + 128].T
    rows = lax.broadcasted_iota(jnp.int32, (B, 128), 0) % 128
    for l in range(KB):
        hot_ref[:, l * 128 : l * 128 + 128] = jnp.where(rows == l, 1.0, 0.0).astype(jnp.bfloat16)

    def lanes(t):
        return slice(t * 128, t * 128 + 128)

    def spread(ref, row, t):
        view = ref.at[row // 8 * 8 : row // 8 * 8 + 8, lanes(t)]
        line = view[pl.ds(row % 8, 8, stride=0), :]
        return jnp.concatenate([line] * (KB // 8), 0)

    def block(k):
        return pl.ds(pl.multiple_of(k, KB), KB)

    def turn(value, k):
        return pltpu.roll(value, lax.rem(128 - lax.rem(k, 128), 128), 1)

    def widen(slot, k, first):
        column = turn(z_refs[first][...], k)
        high = jnp.floor(column * (1 / 32)) * 32
        split = jnp.concatenate([high, column - high], 1).astype(jnp.bfloat16)
        for c in range(0, KB * 128, 512):
            wide_refs[slot][:, c : c + 512] = jnp.dot(split, hot_ref[:, c : c + 512], preferred_element_type=jnp.float32)

    def close(slot, k, first, tiles, beside=None):
        square = turn(old_ref[:, lanes(first)], k)
        for step in range(KB.bit_length() - 1):
            square_ref[step] = square
            left = square[:, :KB]
            for l in range(KB):
                square = jnp.minimum(square, left[:, l : l + 1] + spread(square_ref.at[step], l, 0))
            if beside is not None:
                square = jnp.minimum(square, beside(step) + 8192.0)
        values = [old_ref[:, lanes(t)] for t in tiles]
        for l in range(KB):
            column = jnp.broadcast_to(square[:, l : l + 1], (KB, 128))
            values = [jnp.minimum(v, column + spread(old_ref, l, t)) for v, t in zip(values, tiles)]
        for v, t in zip(values, tiles):
            panel_refs[slot][:, lanes(t)] = v

    def through(slot, starts, tiles):
        values = [[z_refs[t][block(r), :] for t in tiles] for r in starts]
        for l in range(KB):
            lines = [spread(panel_refs[slot], l, t) for t in tiles]
            for n, r in enumerate(starts):
                column = wide_refs[slot][block(r), lanes(l)]
                values[n] = [jnp.minimum(v, column + line) for v, line in zip(values[n], lines)]
        return values

    def update(slot, starts, tiles):
        for r, row in zip(starts, through(slot, starts, tiles)):
            for t, value in zip(tiles, row):
                z_refs[t][block(r), :] = value
        return value

    right = list(range(left_strips, strips))

    def stage(slot, k, first, others):
        after = k + KB
        rest = [lax.rem(after + r, B) for r in range(KB, B - KB, KB)]
        live = [first] + others
        for t, value in zip(live, through(slot, [after], live)[0]):
            old_ref[:, lanes(t)] = value
        update(slot, rest, [first])

        def beside(step):
            tokens = [update(slot, [r], others) for r in rest[3 * step : 3 * step + 3]]
            return functools.reduce(jnp.minimum, tokens)

        widen(1 - slot, after, first)
        close(1 - slot, after, first, live, beside)
        for r in rest[3 * (KB.bit_length() - 1) :]:
            update(slot, [r], others)
        for t in live:
            z_refs[t][block(after), :] = panel_refs[1 - slot][:, lanes(t)]

    def pair(start, first, others):
        def run(i, carry):
            k = start + i * (2 * KB)
            stage(1, k, first, others)
            stage(0, k + KB, first, others)
            return carry

        return run

    widen(0, 0, 0)
    for t in range(strips):
        old_ref[:, lanes(t)] = z_refs[t][0:KB, :]
    close(0, 0, 0, list(range(strips)))
    for t in range(strips):
        z_refs[t][0:KB, :] = panel_refs[0][:, lanes(t)]
    stage(0, 0, 0, [1] + right)
    lax.fori_loop(0, 3, pair(KB, 0, [1] + right), 0)
    lax.fori_loop(0, 4, pair(128 - KB, 1, right), 0)
    for r in range(0, B - KB, KB):
        update(1, [r], right)
    for t in range(strips - left_strips):
        for r in range(0, B, 128):
            c_ref[t * 128 : t * 128 + 128, r : r + 128] = z_refs[left_strips + t][r : r + 128, :].T


TI, TJ, U = 16, 768, 32


def min_plus(x_ref, y_ref, acc_ref, wide_ref, finished):
    height, depth = x_ref.shape
    breadth = y_ref.shape[1]
    blocks, strips = height // TI, breadth // TJ
    share = U // strips

    def widen(slot, left, l0, columns):
        for u in columns:
            wide_ref[slot, l0 + u] = jnp.broadcast_to(left[:, u : u + 1], (TI, 128))
        return pltpu.roll(left, 128 - U, 1)

    for half in range(depth // 128):

        def first(g, left):
            return widen(0, left, pl.multiple_of(half * 128 + g * U, U), range(U))

        lax.fori_loop(0, 128 // U, first, x_ref[0:TI, half * 128 : half * 128 + 128])

    def block(b, carry):
        slot = lax.rem(b, 2)
        row0 = pl.multiple_of(b * TI, TI)
        next0 = pl.multiple_of(jnp.minimum(b + 1, blocks - 1) * TI, TI)
        for s in range(strips):
            strip = slice(s * TJ, (s + 1) * TJ)
            value = acc_ref[pl.ds(row0, TI), strip]
            for half in range(depth // 128):

                def group(g, state):
                    value, left = state
                    l0 = pl.multiple_of(half * 128 + g * U, U)
                    right = y_ref.at[pl.ds(l0, U), strip]
                    for u in range(U):
                        wide = wide_ref[slot, l0 + u]
                        row = right[pl.ds(u, 8, stride=0), :]
                        value = jnp.concatenate(
                            [
                                jnp.minimum(
                                    value[:, c : c + 128], wide + jnp.concatenate([row[:, c : c + 128]] * (TI // 8), 0)
                                )
                                for c in range(0, TJ, 128)
                            ],
                            1,
                        )
                    left = widen(1 - slot, left, l0, range(s * share, s * share + share))
                    return value, left

                left = x_ref[pl.ds(next0, TI), half * 128 : half * 128 + 128]
                value, left = lax.fori_loop(0, 128 // U, group, (value, left))
            acc_ref[pl.ds(row0, TI), strip] = value
        finished(pl.ds(row0, TI), b)
        return carry

    lax.fori_loop(0, blocks, block, 0)


def update_kernel(
    c_ref, p_ref, r_hbm, d_hbm, out_hbm, x_ref, old_ref, square_ref, hot_ref, wide_ref, r_ref, d_ref, sem, out_sem, *more
):
    r_copy = pltpu.make_async_copy(r_hbm, r_ref, sem.at[0])
    d_copy = pltpu.make_async_copy(d_hbm, d_ref, sem.at[1])
    r_copy.start()
    d_copy.start()
    x_ref[...] = c_ref[...]
    close_and_extend(p_ref, x_ref, more[4:], more[:2], more[2:4], old_ref, square_ref, hot_ref)
    r_copy.wait()
    d_copy.wait()

    def put(rows, b):
        return pltpu.make_async_copy(d_ref.at[rows, :], out_hbm.at[rows, :], out_sem.at[b])

    min_plus(x_ref, r_ref, d_ref, wide_ref, lambda rows, b: put(rows, b).start())

    @pl.loop(0, d_ref.shape[0] // TI)
    def _(b):
        put(pl.ds(pl.multiple_of(b * TI, TI), TI), b).wait()


def scratch(rows, cols):
    f32 = jnp.float32
    width = B + rows
    return [
        pltpu.VMEM((rows, B), f32),
        pltpu.VMEM((KB, width), f32),
        pltpu.VMEM((KB.bit_length(), KB, 128), f32),
        pltpu.VMEM((B, KB * 128), jnp.bfloat16),
        pltpu.VMEM((2, B, TI, 128), f32),
        pltpu.VMEM((B, cols), f32),
        pltpu.VMEM((rows, cols), f32),
        pltpu.SemaphoreType.DMA((2,)),
        pltpu.SemaphoreType.DMA((rows // TI,)),
        *[pltpu.VMEM((B, KB * 128), f32)] * 2,
        *[pltpu.VMEM((KB, width), f32)] * 2,
        *[pltpu.VMEM((B, 128), f32)] * (width // 128),
    ]


def on_device(distances):
    rows, cols = distances.shape
    f32 = jnp.float32
    c, r, p = gather(distances)
    return pl.pallas_call(
        update_kernel,
        out_shape=jax.ShapeDtypeStruct((rows, cols), f32),
        in_specs=[pl.BlockSpec(memory_space=pltpu.VMEM)] * 2 + [pl.BlockSpec(memory_space=pl.ANY)] * 2,
        out_specs=pl.BlockSpec(memory_space=pl.ANY),
        scratch_shapes=scratch(rows, cols),
        name="update",
    )(c, p, r, distances)


def solution(mesh):
    spec = P("row", "col")
    return jax.shard_map(on_device, mesh=mesh, in_specs=(spec,), out_specs=spec, check_vma=False)
```
